32 devices in a mesh: row: 4 (over y, x), col: 8 (over z, core).
Axes of the slice: x: 2, y: 2, z: 4, core: 2. Of those that a mesh axis runs over, the one named last changes fastest.
Arguments:
- inputs: bfloat16 [2048, 25600], P('row', 'col'), may hold values from -6 to 6
- out_grads: bfloat16 [2048, 5120], P('col', 'row'), may hold values from -0.125 to 0.125
- weights: bfloat16 [5120, 25600], P('row', 'col'), may hold values from -3 to 3
- momentum: float32 [5120, 25600], P('row', 'col'), may hold values from -13 to 13
- right_factor: float32 [25600, 256], P('col'), may hold values from -6 to 6
Outputs:
- weights_new: float32 [5120, 25600], P('row', 'col')
- momentum_new: float32 [5120, 25600], P('row', 'col')
- factor_new: float32 [25600, 256], P('col')
The draws below stay inside these ranges and needn't reach their ends.
All inputs are finite; a program needn't handle non-finite values.
Results may differ from the reference program's by a relative error of at most 0.0003.
Values may be sent and summed in bfloat16 or wider, within the bound.
No kernel may reach another device: no remote copies, remote signals or barrier semaphores. Data moves between devices by JAX's collectives and lax.ppermute only.
A program may use at most 128 MiB of HBM per device.

```python
import math
import jax
import jax.numpy as jnp
from jax import lax

M = 5120
N = 25600
RANK = 256
TOKENS = 2048


def draw_momentum(key, part):
    keys = jax.random.split(jax.random.fold_in(key, 7), 3)
    row_scale = jnp.exp(jax.random.uniform(keys[0], (M, 1), jnp.float32, -0.58, 0.58))
    col_scale = jnp.exp(jax.random.uniform(keys[1], (1, N), jnp.float32, -0.58, 0.58))
    base = jnp.clip(jax.random.normal(keys[2], (M, N), jnp.float32), -4.0, 4.0)
    return base * row_scale * col_scale


def block_scale(own_key, shape, cuts, low, largest):
    level, own = 1.0, jax.random.fold_in(own_key, 6)
    for axis_at, blocks in cuts:
        draws = jnp.exp(jax.random.uniform(jax.random.fold_in(own, axis_at), (blocks,), jnp.float32, low / len(cuts), largest / len(cuts)))
        level = level * jnp.repeat(draws, shape[axis_at] // blocks).reshape([-1 if axis == axis_at else 1 for axis in range(len(shape))])
    return level


def scatter_about(own_key, extent, deviation, most, cuts=(), dtype=jnp.bfloat16):
    level = block_scale(own_key, extent, cuts, -0.22, 0.18) if cuts else 1.0
    result = jax.random.normal(own_key, extent, jnp.float32) * deviation * level
    return jnp.minimum(jnp.maximum(result, -most), most).astype(dtype)


def setup_inputs(seed: int = 0) -> dict:
    arg_keys = jax.random.split(jax.random.key(seed), 6)
    return {
        "inputs": scatter_about(arg_keys[0], (TOKENS, N), 1.0, 6.0, ((0, 4), (1, 8))),
        "out_grads": scatter_about(arg_keys[1], (TOKENS, M), TOKENS ** -0.5, 0.125, ((0, 8), (1, 4))),
        "weights": scatter_about(arg_keys[2], (M, N), 0.5, 3.0, ((0, 4), (1, 8))),
        "momentum": draw_momentum(jax.random.fold_in(arg_keys[5], 71), 0),
        "right_factor": scatter_about(arg_keys[4], (N, RANK), 1.0, 6.0, ((0, 8),), jnp.float32),
    }


mix_rate = 0.95
step_rate = 0.3
weight_decay = 0.1
tiny_eps = 1e-06
highest = lax.Precision.HIGHEST

def reference(inputs, out_grads, weights, momentum, right_factor):
    gradient = jnp.dot(out_grads.T.astype(jnp.float32), inputs.astype(jnp.float32), preferred_element_type=jnp.float32)
    moment = momentum + gradient
    sketch = jnp.dot(moment, right_factor, precision=highest)
    gram = jnp.dot(sketch.T, sketch, precision=highest)
    factor_low = jnp.linalg.cholesky(gram)
    basis = jax.scipy.linalg.solve_triangular(factor_low, sketch.T, lower=True).T
    right_side = jnp.dot(moment.T, basis, precision=highest)
    column_scale = lax.rsqrt(lax.optimization_barrier(jnp.sum(right_side * right_side, axis=0)) / N + tiny_eps)
    factor_new = right_side * column_scale
    momentum_new = moment - (1.0 - mix_rate) * jnp.dot(basis, right_side.T, precision=highest)
    update = jnp.dot(basis, factor_new.T, precision=highest)
    weights_new = weights.astype(jnp.float32) * (1.0 - step_rate * weight_decay) - step_rate * math.sqrt(M / RANK) * update
    return (weights_new, momentum_new, factor_new)
```

```python
import functools
import math

import jax
import jax.numpy as jnp
from jax import lax
from jax.experimental import pallas as pl
from jax.experimental.pallas import tpu as pltpu
from jax.sharding import PartitionSpec as P


mix_rate = 0.95
step_rate = 0.3
weight_decay = 0.1
tiny_eps = 1e-06
highest = lax.Precision.HIGHEST
high = lax.Precision.HIGH
f32 = jnp.float32


def mm(a, b, dims, precision=None):
    return lax.dot_general(a, b, (dims, ((), ())), precision=precision, preferred_element_type=f32)


def general(n_total, m_total, inputs, out_grads, weights, momentum, right_factor):
    rank = right_factor.shape[1]
    grads_all = lax.all_gather(out_grads, "col", axis=0, tiled=True)
    inputs_all = lax.all_gather(inputs, "row", axis=0, tiled=True)
    moment = momentum + mm(grads_all, inputs_all, ((0,), (0,)))
    sketch = lax.psum(mm(moment, right_factor, ((1,), (0,)), highest), "col")
    gram = lax.psum(mm(sketch, sketch, ((0,), (0,)), highest), "row")
    inverse = inverse_factor(gram)
    basis = mm(sketch, inverse, ((1,), (1,)), highest)
    right_side = lax.psum(mm(moment, basis, ((0,), (0,)), highest), "row")
    squares = lax.psum(jnp.sum(right_side * right_side, axis=0), "col")
    factor_new = right_side * lax.rsqrt(squares / n_total + tiny_eps)
    momentum_new = moment - (1.0 - mix_rate) * mm(basis, right_side, ((1,), (1,)), highest)
    update = mm(basis, factor_new, ((1,), (1,)), highest)
    weights_new = (
        weights.astype(f32) * (1.0 - step_rate * weight_decay)
        - step_rate * math.sqrt(m_total / rank) * update
    )
    return (weights_new, momentum_new, factor_new)


def base_inverse(a):
    n = a.shape[0]
    rows = lax.broadcasted_iota(jnp.int32, (n, n), 0)
    cols = lax.broadcasted_iota(jnp.int32, (n, n), 1)
    left = a
    right = jnp.where(rows == cols, 1.0, 0.0).astype(f32)
    pivots = jnp.ones((n, n), f32)
    step = 8
    for start in range(0, n, step):
        columns = [jnp.broadcast_to(left[:, start + i : start + i + 1], (n, n)) for i in range(step)]
        for i in range(step):
            j = start + i
            pivot = jnp.broadcast_to(columns[i][j : j + 1, :], (n, n))
            pivots = jnp.where(rows == j, pivot, pivots)
            if j + 1 == n:
                break
            ratio = jnp.where(rows > j, columns[i] * (1.0 / pivot), 0.0)
            for k in range(i + 1, step):
                columns[k] = columns[k] - ratio * jnp.broadcast_to(columns[k][j : j + 1, :], (n, n))
            left = left - ratio * jnp.broadcast_to(left[j : j + 1, :], (n, n))
            right = right - ratio * jnp.broadcast_to(right[j : j + 1, :], (n, n))
    root = lax.rsqrt(pivots)
    return right * (root * (1.5 - 0.5 * pivots * root * root))


def inverse_kernel(gram_ref, out_ref, work_ref):
    n = gram_ref.shape[0]
    work_ref[...] = gram_ref[...]
    out_ref[...] = jnp.zeros_like(out_ref)

    def solve(at, size):
        span = slice(at, at + size)
        if size <= 32:
            out_ref[span, span] = base_inverse(work_ref[span, span])
            return
        half = size // 2
        one, two = slice(at, at + half), slice(at + half, at + size)
        solve(at, half)
        inv_one = out_ref[one, one]
        low = mm(work_ref[two, one], inv_one, ((1,), (1,)), highest)
        work_ref[two, two] = work_ref[two, two] - mm(low, low, ((1,), (1,)), highest)
        side = mm(low, inv_one, ((1,), (0,)), highest)
        solve(at + half, half)
        out_ref[two, one] = -mm(out_ref[two, two], side, ((1,), (0,)), highest)

    solve(0, n)


def inverse_factor(gram):
    return pl.pallas_call(
        inverse_kernel,
        out_shape=jax.ShapeDtypeStruct(gram.shape, f32),
        in_specs=[pl.BlockSpec(memory_space=pltpu.VMEM)],
        out_specs=pl.BlockSpec(memory_space=pltpu.VMEM),
        scratch_shapes=[pltpu.VMEM(gram.shape, f32)],
        name="inverse_factor",
        cost_estimate=pl.CostEstimate(flops=20_000_000_000, bytes_accessed=10_000_000, transcendentals=0),
    )(gram)


bf16 = jnp.bfloat16
whole_vmem = pl.BlockSpec(memory_space=pltpu.VMEM)
whole_smem = pl.BlockSpec(memory_space=pltpu.SMEM)


def split(x):
    big = x.astype(bf16)
    return big, (x - big.astype(f32)).astype(bf16)


def tile_of(n):
    return 640 if n % 640 == 0 else n


def call(kernel, outs, ins, specs, out_specs, grid=(), scratch=(), flops=0, moved=0, aliases={}):
    return pl.pallas_call(
        kernel,
        out_shape=outs,
        grid=grid,
        in_specs=specs,
        out_specs=out_specs,
        scratch_shapes=list(scratch),
        input_output_aliases=aliases,
        compiler_params=pltpu.CompilerParams(dimension_semantics=("arbitrary",) * len(grid)),
        cost_estimate=pl.CostEstimate(flops=flops, bytes_accessed=moved, transcendentals=0),
    )(*ins)


def shaped(shape, dtype=f32):
    return jax.ShapeDtypeStruct(shape, dtype)


def sketch_kernel(ids, part, *refs):
    grads, rights, keep, send, big, low = refs[:4], refs[4:8], refs[8], refs[9], refs[10], refs[11]
    z, core, shift = ids[1], ids[2], ids[3]
    for k in range(4):
        big[k], low[k] = split(rights[k][...])
    rows = keep.shape[0] // 4
    for out, half in ((keep, core), (send, 1 - core)):
        for b in range(4):
            at = pl.ds(pl.multiple_of(half * (4 * rows) + (z ^ b) * rows, 32), rows)
            total = part[at, :]
            for k in range(4):
                g = grads[k][at, :]
                total += mm(g, big[k ^ shift], ((1,), (0,)))
                total += mm(g, low[k ^ shift], ((1,), (0,)))
            out[b * rows : (b + 1) * rows, :] = total


def gram_kernel(ids, *refs):
    parts, other, grads = refs[:4], refs[4], refs[5:9]
    sketch, gram, tokens, big_t, low_t, flip = refs[9:]
    row, z, core, shift = ids[0], ids[1], ids[2], ids[3]
    rows = parts[0].shape[0]
    for k in range(4):
        at = pl.multiple_of((z ^ k) * rows, 32)
        sketch[pl.ds(core * (4 * rows) + at, rows), :] = parts[k][...]
        sketch[pl.ds((1 - core) * (4 * rows) + at, rows), :] = other[k * rows : (k + 1) * rows, :]
    s = sketch[...]
    gram[...] = mm(s, s, ((0,), (0,)), highest)
    big, low = split(s)
    for k in range(4):
        g = grads[k][...]
        tokens[k ^ shift] = mm(g, big, ((0,), (0,))) + mm(g, low, ((0,), (0,)))
    flip[...] = s.T
    size = flip.shape[0] // 8
    for i in range(8):
        at = pl.multiple_of(rank_block(row, i) * size, 32)
        b, l = split(flip[pl.ds(at, size), :])
        big_t[i * size : (i + 1) * size, :] = b
        low_t[i * size : (i + 1) * size, :] = l


def rank_block(row, i):
    bit_x, bit_y = row % 2, row // 2
    upper, lower = (i // 2) % 2, i % 2
    if i < 4:
        return 2 * (upper ^ bit_x) + (lower ^ bit_y)
    return 4 + 2 * (upper ^ bit_y) + (lower ^ bit_x)


def side_kernel(big_t, low_t, momentum, top_keep, top_send, low_keep, low_send):
    mb, ml = split(momentum[...])
    total = mm(big_t[...], mb, ((1,), (0,)))
    total += mm(big_t[...], ml, ((1,), (0,)))
    total += mm(low_t[...], mb, ((1,), (0,)))
    n = top_keep.shape[0]
    for i, ref in enumerate((top_keep, top_send, low_keep, low_send)):
        ref[...] = total[i * n : (i + 1) * n, :]


def token_kernel(ids, own, other, inputs, *refs):
    before, after_refs, flip, tok = refs[:4], refs[4:8], refs[8], refs[9]
    row, core = ids[0], ids[2]
    half = own.shape[0]
    size = flip.shape[0] // 8

    @pl.when(pl.program_id(0) == 0)
    def _():
        for ref, place in ((own, core), (other, 1 - core)):
            flip[...] = ref[...].T
            for i in range(8):
                at = pl.multiple_of(rank_block(row, i) * size, 32)
                b, l = split(flip[pl.ds(at, size), :])
                tok[place, 0, i * size : (i + 1) * size, :] = b
                tok[place, 1, i * size : (i + 1) * size, :] = l

    total = 0.0
    for h in range(2):
        x = inputs[h * half : (h + 1) * half, :]
        total += mm(tok[h, 0], x, ((1,), (0,)))
        total += mm(tok[h, 1], x, ((1,), (0,)))
    n = after_refs[0].shape[0]
    for i in range(4):
        after_refs[i][...] = before[i][...] + total[i * n : (i + 1) * n, :]


def gradient_kernel(count, ids, *refs):
    own, other, blocks, base, out = refs[:count], refs[count : 2 * count], refs[2 * count : 3 * count], refs[3 * count], refs[3 * count + 1]
    core = ids[2]
    half = blocks[0].shape[0] // 2
    total = base[...]
    for mine, its, x in zip(own, other, blocks):
        at = pl.multiple_of(core * half, half)
        total += mm(mine[0], x[pl.ds(at, half), :], ((1,), (0,)))
        at = pl.multiple_of((1 - core) * half, half)
        total += mm(its[0], x[pl.ds(at, half), :], ((1,), (0,)))
    out[...] = total


def right_kernel(ids, inverse, sketch, *refs):
    pieces, right, squares, basis, work = refs[:6], refs[6], refs[7], refs[8], refs[9]
    row = ids[0]
    size = work.shape[0] // 8

    @pl.when(pl.program_id(0) == 0)
    def _():
        sb, sl = split(sketch[...])
        ib, il = split(inverse[...])
        basis[...] = mm(sb, ib, ((1,), (1,))) + mm(sb, il, ((1,), (1,))) + mm(sl, ib, ((1,), (1,)))
        squares[...] = jnp.zeros_like(squares)

    place = 0
    for ref in pieces:
        for i in range(ref.shape[0] // size):
            at = pl.multiple_of(rank_block(row, place) * size, 32)
            work[pl.ds(at, size), :] = ref[i * size : (i + 1) * size, :]
            place += 1
    ib, il = split(inverse[...])
    tb, tl = split(work[...])
    total = mm(ib, tb, ((1,), (0,))) + mm(ib, tl, ((1,), (0,))) + mm(il, tb, ((1,), (0,)))
    right[...] = total
    sb, sl = split(total * total)
    ones = jnp.ones((8, total.shape[1]), bf16)
    squares[...] += mm(ones, sb, ((1,), (1,))) + mm(ones, sl, ((1,), (1,)))


def weights_kernel(n_total, factor, squares, basis, right, weights, out, factor_out, big, low):
    scale = lax.rsqrt(squares[0:1, :] / n_total + tiny_eps)

    @pl.when(pl.program_id(0) == 0)
    def _():
        big[...], low[...] = split(basis[...] * (scale * -factor))

    rb, rl = split(right[...])
    update = mm(big[...], rb, ((1,), (0,))) + mm(big[...], rl, ((1,), (0,))) + mm(low[...], rb, ((1,), (0,)))
    out[...] = weights[...].astype(f32) * (1.0 - step_rate * weight_decay) + update
    factor_out[...] = right[...].T * scale


def momentum_kernel(ids, own, other, first, second, basis, right, base, out, table, small):
    core = ids[2]

    @pl.when(pl.program_id(0) == 0)
    def _():
        table[core] = own[0]
        table[1 - core] = other[0]
        small[...] = (basis[...] * -(1.0 - mix_rate)).astype(bf16)

    total = base[...]
    total += mm(table[0], first[...], ((1,), (0,)))
    total += mm(table[1], second[...], ((1,), (0,)))
    total += mm(small[...], right[...].astype(bf16), ((1,), (0,)))
    out[...] = total


def swap(x, axis, bit):
    size = lax.axis_size(axis)
    return lax.ppermute(x, axis, [(i, i ^ bit) for i in range(size)])


def plane(n_total, m_total, inputs, out_grads, weights, momentum, right_factor):
    return plane_body(n_total, m_total, inputs, out_grads, weights, momentum, right_factor)


def plane_body(n_total, m_total, inputs, out_grads, weights, momentum, right_factor):
    rank = right_factor.shape[1]
    row = lax.axis_index("row")
    col = lax.axis_index("col")
    core, z = col % 2, col // 2
    ids = jnp.stack([row, z, core, row ^ z]).astype(jnp.int32)
    tokens, n = inputs.shape
    m = momentum.shape[0]
    block = out_grads.shape[0]
    tn = tile_of(n)
    quarter = [1, 2, 3]
    tiles = (n // tn,)

    def columns(rows):
        return pl.BlockSpec((rows, tn), lambda i: (0, i))

    grads = out_grads.T
    own = [grads] + [swap(grads, "col", 2 * k) for k in quarter]

    in_right = mm(inputs.astype(f32), right_factor, ((1,), (0,)), high)
    flipped = jnp.where(core == 0, 0, 1)
    keep = lax.dynamic_slice_in_dim(in_right, flipped * block, block, 0)
    send = lax.dynamic_slice_in_dim(in_right, (1 - flipped) * block, block, 0)
    in_right = keep + swap(send, "col", 1)
    rights = [in_right] + [swap(in_right, "row", k) for k in quarter]
    x_all = swap(inputs, "row", 1)
    y_all = swap(inputs, "row", 2)
    other = [swap(g, "col", 1) for g in own]

    part = mm(momentum, right_factor, ((1,), (0,)), high)
    keep, send = call(
        sketch_kernel, (shaped((m // 2, rank)),) * 2, (ids, part, *own, *rights),
        [whole_smem] + [whole_vmem] * 9, (whole_vmem,) * 2,
        scratch=[pltpu.VMEM((4, block, rank), bf16)] * 2, flops=4 * m * 4 * block * rank, moved=8_000_000)
    mine = keep + swap(send, "col", 1)
    size = m // 8
    total = mine[:size]
    for k in quarter:
        total = total + swap(mine[k * size : (k + 1) * size], "col", 2 * k)
    parts = [total] + [swap(total, "col", 2 * k) for k in quarter]
    rest = swap(jnp.concatenate(parts, axis=0), "col", 1)

    sketch, gram, toks, big_t, low_t = call(
        gram_kernel,
        (shaped((m, rank)), shaped((rank, rank)), shaped((4, block, rank)), shaped((rank, m), bf16), shaped((rank, m), bf16)),
        (ids, *parts, rest, *own), [whole_smem] + [whole_vmem] * 9, (whole_vmem,) * 5,
        scratch=[pltpu.VMEM((rank, m), f32)], flops=20 * m * rank * rank, moved=8_000_000)
    token = toks[0]
    for k in quarter:
        token = token + swap(toks[k], "row", k)
    token_other = swap(token, "col", 1)
    gram = gram + swap(gram, "row", 1)
    gram = gram + swap(gram, "row", 2)

    sides = call(
        side_kernel, (shaped((rank // 4, n)),) * 4, (big_t, low_t, momentum),
        [whole_vmem] * 2 + [columns(m)], (columns(rank // 4),) * 4, tiles,
        flops=6 * m * n * rank, moved=5 * m * n)
    top, top_send, low, low_send = call(
        token_kernel, (shaped((rank // 4, n)),) * 4,
        (ids, token, token_other, inputs, *sides),
        [whole_smem] + [whole_vmem] * 2 + [columns(tokens)] + [columns(rank // 4)] * 4, (columns(rank // 4),) * 4, tiles,
        scratch=[pltpu.VMEM((rank, block), f32), pltpu.VMEM((2, 2, rank, block), bf16)],
        flops=4 * tokens * n * rank, moved=10 * rank * n, aliases={4: 0, 5: 1, 6: 2, 7: 3})
    n8 = rank // 8
    top = top + swap(top_send, "row", 1)
    low = low + swap(low_send, "row", 2)
    top0 = top[:n8] + swap(top[n8:], "row", 2)
    low0 = low[:n8] + swap(low[n8:], "row", 1)
    top1 = swap(top0, "row", 2)
    low1 = swap(low0, "row", 1)
    top2 = swap(jnp.concatenate([top0, top1], axis=0), "row", 1)
    low2 = swap(jnp.concatenate([low0, low1], axis=0), "row", 2)

    inverse = inverse_factor(gram)
    half = tokens // 2
    d_first = swap(x_all[:half], "row", 2)
    d_second = swap(y_all[half:], "row", 1)

    own_all = jnp.stack(own)
    other_all = jnp.stack(other)

    def pick(j):
        return pl.BlockSpec((1, m, block), lambda i, ids: (ids[3] ^ j, 0, 0))

    def cols(rows):
        return pl.BlockSpec((rows, tn), lambda i, ids: (0, i))

    moment = pl.pallas_call(
        functools.partial(gradient_kernel, 3),
        grid_spec=pltpu.PrefetchScalarGridSpec(
            num_scalar_prefetch=1, grid=tiles,
            in_specs=[pick(0), pick(1), pick(2)] * 2 + [cols(tokens)] * 3 + [cols(m)],
            out_specs=cols(m)),
        out_shape=shaped((m, n)), name="gradient",
        cost_estimate=pl.CostEstimate(flops=6 * m * n * tokens, bytes_accessed=8 * m * n, transcendentals=0),
    )(ids, *([own_all] * 3), *([other_all] * 3), inputs, x_all, y_all, momentum)

    right, squares, basis = call(
        right_kernel, (shaped((rank, n)), shaped((8, rank)), shaped((m, rank))),
        (ids, inverse, sketch, top0, top1, top2, low0, low1, low2),
        [whole_smem] + [whole_vmem] * 2 + [columns(n8), columns(n8), columns(2 * n8)] * 2,
        (columns(rank), pl.BlockSpec((8, rank), lambda i: (0, 0)), pl.BlockSpec((m, rank), lambda i: (0, 0))), tiles,
        scratch=[pltpu.VMEM((rank, tn), f32)], flops=6 * n * rank * rank, moved=12 * n * rank)
    for bit in (1, 2, 4):
        squares = squares + swap(squares, "col", bit)
    weights_new, factor_new = call(
        functools.partial(weights_kernel, n_total, step_rate * math.sqrt(m_total / rank)),
        (shaped((m, n)), shaped((n, rank))), (squares, basis, right, weights),
        [whole_vmem] * 2 + [columns(rank), columns(m)],
        (columns(m), pl.BlockSpec((tn, rank), lambda i: (i, 0))), tiles,
        scratch=[pltpu.VMEM((m, rank), bf16)] * 2, flops=6 * m * n * rank, moved=6 * m * n)
    momentum_new = pl.pallas_call(
        momentum_kernel,
        grid_spec=pltpu.PrefetchScalarGridSpec(
            num_scalar_prefetch=1, grid=tiles,
            in_specs=[pick(3), pick(3), cols(half), cols(half), pl.BlockSpec((m, rank), lambda i, ids: (0, 0)), cols(rank), cols(m)],
            out_specs=cols(m),
            scratch_shapes=[pltpu.VMEM((2, m, block), bf16), pltpu.VMEM((m, rank), bf16)]),
        out_shape=shaped((m, n)), name="momentum", input_output_aliases={7: 0},
        cost_estimate=pl.CostEstimate(flops=2 * m * n * (tokens + rank), bytes_accessed=8 * m * n, transcendentals=0),
    )(ids, own_all, other_all, d_first, d_second, basis, right, moment)
    return (weights_new, momentum_new, factor_new)


def solution(mesh):
    n_row, n_col = mesh.shape["row"], mesh.shape["col"]
    fast = (n_row, n_col) == (4, 8)
    body = plane if fast else general

    def whole(inputs, out_grads, weights, momentum, right_factor):
        m_total, n_total = weights.shape
        return jax.shard_map(
            functools.partial(body, n_total, m_total),
            mesh=mesh,
            in_specs=(P("row", "col"), P("col", "row"), P("row", "col"), P("row", "col"), P("col", None)),
            out_specs=(P("row", "col"), P("row", "col"), P("col", None)),
            check_vma=False,
        )(inputs, out_grads, weights, momentum, right_factor)

    return whole
```

```python
import functools
import math

import jax
import jax.numpy as jnp
from jax import lax
from jax.experimental import pallas as pl
from jax.experimental.pallas import tpu as pltpu
from jax.sharding import PartitionSpec as P


mix_rate = 0.95
step_rate = 0.3
weight_decay = 0.1
tiny_eps = 1e-06
highest = lax.Precision.HIGHEST
high = lax.Precision.HIGH
f32 = jnp.float32


def mm(a, b, dims, precision=None):
    return lax.dot_general(a, b, (dims, ((), ())), precision=precision, preferred_element_type=f32)


def general(n_total, m_total, inputs, out_grads, weights, momentum, right_factor):
    rank = right_factor.shape[1]
    grads_all = lax.all_gather(out_grads, "col", axis=0, tiled=True)
    inputs_all = lax.all_gather(inputs, "row", axis=0, tiled=True)
    moment = momentum + mm(grads_all, inputs_all, ((0,), (0,)))
    sketch = lax.psum(mm(moment, right_factor, ((1,), (0,)), highest), "col")
    gram = lax.psum(mm(sketch, sketch, ((0,), (0,)), highest), "row")
    inverse = inverse_factor(gram)
    basis = mm(sketch, inverse, ((1,), (1,)), highest)
    right_side = lax.psum(mm(moment, basis, ((0,), (0,)), highest), "row")
    squares = lax.psum(jnp.sum(right_side * right_side, axis=0), "col")
    factor_new = right_side * lax.rsqrt(squares / n_total + tiny_eps)
    momentum_new = moment - (1.0 - mix_rate) * mm(basis, right_side, ((1,), (1,)), highest)
    update = mm(basis, factor_new, ((1,), (1,)), highest)
    weights_new = (
        weights.astype(f32) * (1.0 - step_rate * weight_decay)
        - step_rate * math.sqrt(m_total / rank) * update
    )
    return (weights_new, momentum_new, factor_new)


def base_inverse(a):
    n = a.shape[0]
    rows = lax.broadcasted_iota(jnp.int32, (n, n), 0)
    cols = lax.broadcasted_iota(jnp.int32, (n, n), 1)
    left = a
    right = jnp.where(rows == cols, 1.0, 0.0).astype(f32)
    pivots = jnp.ones((n, n), f32)
    step = 8
    for start in range(0, n, step):
        columns = [jnp.broadcast_to(left[:, start + i : start + i + 1], (n, n)) for i in range(step)]
        for i in range(step):
            j = start + i
            pivot = jnp.broadcast_to(columns[i][j : j + 1, :], (n, n))
            pivots = jnp.where(rows == j, pivot, pivots)
            if j + 1 == n:
                break
            ratio = jnp.where(rows > j, columns[i] * (1.0 / pivot), 0.0)
            for k in range(i + 1, step):
                columns[k] = columns[k] - ratio * jnp.broadcast_to(columns[k][j : j + 1, :], (n, n))
            left = left - ratio * jnp.broadcast_to(left[j : j + 1, :], (n, n))
            right = right - ratio * jnp.broadcast_to(right[j : j + 1, :], (n, n))
    root = lax.rsqrt(pivots)
    return right * (root * (1.5 - 0.5 * pivots * root * root))


def inverse_kernel(gram_ref, out_ref, work_ref):
    n = gram_ref.shape[0]
    work_ref[...] = gram_ref[...]
    out_ref[...] = jnp.zeros_like(out_ref)

    def solve(at, size):
        span = slice(at, at + size)
        if size <= 32:
            out_ref[span, span] = base_inverse(work_ref[span, span])
            return
        half = size // 2
        one, two = slice(at, at + half), slice(at + half, at + size)
        solve(at, half)
        inv_one = out_ref[one, one]
        low = mm(work_ref[two, one], inv_one, ((1,), (1,)), highest)
        work_ref[two, two] = work_ref[two, two] - mm(low, low, ((1,), (1,)), highest)
        side = mm(low, inv_one, ((1,), (0,)), highest)
        solve(at + half, half)
        out_ref[two, one] = -mm(out_ref[two, two], side, ((1,), (0,)), highest)

    solve(0, n)


def inverse_factor(gram):
    return pl.pallas_call(
        inverse_kernel,
        out_shape=jax.ShapeDtypeStruct(gram.shape, f32),
        in_specs=[pl.BlockSpec(memory_space=pltpu.VMEM)],
        out_specs=pl.BlockSpec(memory_space=pltpu.VMEM),
        scratch_shapes=[pltpu.VMEM(gram.shape, f32)],
        cost_estimate=pl.CostEstimate(flops=20_000_000_000, bytes_accessed=10_000_000, transcendentals=0),
    )(gram)


bf16 = jnp.bfloat16
whole_vmem = pl.BlockSpec(memory_space=pltpu.VMEM)
whole_smem = pl.BlockSpec(memory_space=pltpu.SMEM)


def split(x):
    big = x.astype(bf16)
    return big, (x - big.astype(f32)).astype(bf16)


def tile_of(n):
    return min(n, 512)


def call(kernel, outs, ins, specs, out_specs, grid=(), scratch=(), flops=0, moved=0, aliases={}, prefetch=0):
    return pl.pallas_call(
        kernel,
        out_shape=outs,
        grid_spec=pltpu.PrefetchScalarGridSpec(
            num_scalar_prefetch=prefetch, grid=grid, in_specs=specs, out_specs=out_specs, scratch_shapes=list(scratch)
        ),
        input_output_aliases=aliases,
        cost_estimate=pl.CostEstimate(flops=flops, bytes_accessed=moved, transcendentals=0),
    )(*ins)


def shaped(shape, dtype=f32):
    return jax.ShapeDtypeStruct(shape, dtype)


def sketch_kernel(ids, part, *refs):
    grads, rights, keep, send, big, low = refs[:4], refs[4:8], refs[8], refs[9], refs[10], refs[11]
    z, core, shift = ids[1], ids[2], ids[3]
    for k in range(4):
        big[k], low[k] = split(rights[k][...])
    rows = keep.shape[0] // 4
    for out, half in ((keep, core), (send, 1 - core)):
        for b in range(4):
            at = pl.ds(pl.multiple_of(half * (4 * rows) + (z ^ b) * rows, 32), rows)
            total = part[at, :]
            for k in range(4):
                g = grads[k][at, :]
                total += mm(g, big[k ^ shift], ((1,), (0,)))
                total += mm(g, low[k ^ shift], ((1,), (0,)))
            out[b * rows : (b + 1) * rows, :] = total


def gram_kernel(ids, *refs):
    parts, other, grads = refs[:4], refs[4], refs[5:9]
    sketch, gram, tokens, big_t, low_t, flip = refs[9:]
    row, z, core, shift = ids[0], ids[1], ids[2], ids[3]
    rows = parts[0].shape[0]
    for k in range(4):
        at = pl.multiple_of((z ^ k) * rows, 32)
        sketch[pl.ds(core * (4 * rows) + at, rows), :] = parts[k][...]
        sketch[pl.ds((1 - core) * (4 * rows) + at, rows), :] = other[k * rows : (k + 1) * rows, :]
    s = sketch[...]
    gram[...] = mm(s, s, ((0,), (0,)), highest)
    big, low = split(s)
    for k in range(4):
        g = grads[k][...]
        tokens[k ^ shift] = mm(g, big, ((0,), (0,))) + mm(g, low, ((0,), (0,)))
    flip[...] = s.T
    size = flip.shape[0] // 8
    for i in range(8):
        at = pl.multiple_of(rank_block(row, i) * size, 32)
        b, l = split(flip[pl.ds(at, size), :])
        big_t[i * size : (i + 1) * size, :] = b
        low_t[i * size : (i + 1) * size, :] = l


def rank_block(row, i):
    bit_x, bit_y = row % 2, row // 2
    upper, lower = (i // 2) % 2, i % 2
    if i < 4:
        return 2 * (upper ^ bit_x) + (lower ^ bit_y)
    return 4 + 2 * (upper ^ bit_y) + (lower ^ bit_x)


def side_kernel(big_t, low_t, momentum, top_keep, top_send, low_keep, low_send):
    mb, ml = split(momentum[...])
    total = mm(big_t[...], mb, ((1,), (0,)))
    total += mm(big_t[...], ml, ((1,), (0,)))
    total += mm(low_t[...], mb, ((1,), (0,)))
    n = top_keep.shape[0]
    for i, ref in enumerate((top_keep, top_send, low_keep, low_send)):
        ref[...] = total[i * n : (i + 1) * n, :]


def token_kernel(ids, own, other, inputs, *refs):
    before, after_refs, flip, tok = refs[:4], refs[4:10], refs[10], refs[11]
    row, core = ids[0], ids[2]
    half = own.shape[0]
    size = flip.shape[0] // 8

    @pl.when(pl.program_id(0) == 0)
    def _():
        for ref, place in ((own, core), (other, 1 - core)):
            flip[...] = ref[...].T
            for i in range(8):
                at = pl.multiple_of(rank_block(row, i) * size, 32)
                b, l = split(flip[pl.ds(at, size), :])
                tok[place, 0, i * size : (i + 1) * size, :] = b
                tok[place, 1, i * size : (i + 1) * size, :] = l

    total = 0.0
    for h in range(2):
        x = inputs[h * half : (h + 1) * half, :]
        total += mm(tok[h, 0], x, ((1,), (0,)))
        total += mm(tok[h, 1], x, ((1,), (0,)))
    for p in range(2):
        keep, send = before[2 * p], before[2 * p + 1]
        first, second, out = after_refs[3 * p : 3 * p + 3]
        at = 4 * p * size
        first[...] = keep[:size, :] + total[at : at + size, :]
        second[...] = keep[size:, :] + total[at + size : at + 2 * size, :]
        out[...] = send[...] + total[at + 2 * size : at + 4 * size, :]


def gradient_kernel(count, crossing, ids, *refs):
    own, other = refs[:count], refs[count : 2 * count]
    blocks, base, out = refs[2 * count : -2], refs[-2], refs[-1]
    core = ids[2]
    total = base[...]
    for at_block in range(count - crossing):
        x = blocks[at_block]
        half = x.shape[0] // 2
        at = pl.multiple_of(core * half, half)
        total += mm(own[at_block][0], x[pl.ds(at, half), :], ((1,), (0,)))
        at = pl.multiple_of((1 - core) * half, half)
        total += mm(other[at_block][0], x[pl.ds(at, half), :], ((1,), (0,)))
    if crossing:
        total += crossed(core, own[-1], other[-1], blocks[-2], blocks[-1], 0)
    out[...] = total


def crossed(core, own, other, first, second, part):
    size = first.shape[0]
    cut = slice(part * size, (part + 1) * size)
    mine = jnp.where(core == 0, first[...], second[...])
    its = jnp.where(core == 0, second[...], first[...])
    return mm(own[0][:, cut], mine, ((1,), (0,))) + mm(other[0][:, cut], its, ((1,), (0,)))


def right_kernel(n, ids, inverse, sketch, *refs):
    pieces, right, squares, basis, work = refs[:6], refs[6], refs[7], refs[8], refs[9]
    row = ids[0]
    size = work.shape[0] // 8

    @pl.when(pl.program_id(0) == 0)
    def _():
        sb, sl = split(sketch[...])
        ib, il = split(inverse[...])
        basis[...] = mm(sb, ib, ((1,), (1,))) + mm(sb, il, ((1,), (1,))) + mm(sl, ib, ((1,), (1,)))
        squares[...] = jnp.zeros_like(squares)

    place = 0
    for ref in pieces:
        for i in range(ref.shape[0] // size):
            at = pl.multiple_of(rank_block(row, place) * size, 32)
            work[pl.ds(at, size), :] = ref[i * size : (i + 1) * size, :]
            place += 1
    ib, il = split(inverse[...])
    tb, tl = split(work[...])
    total = mm(ib, tb, ((1,), (0,))) + mm(ib, tl, ((1,), (0,))) + mm(il, tb, ((1,), (0,)))
    right[...] = total
    at = pl.program_id(0) * total.shape[1] + lax.broadcasted_iota(jnp.int32, total.shape, 1)
    sb, sl = split(jnp.where(at < n, total * total, 0.0))
    ones = jnp.ones((8, total.shape[1]), bf16)
    squares[...] += mm(ones, sb, ((1,), (1,))) + mm(ones, sl, ((1,), (1,)))


def weights_kernel(n_total, factor, squares, basis, right, weights, out, factor_out, big, low):
    scale = lax.rsqrt(squares[0:1, :] / n_total + tiny_eps)

    @pl.when(pl.program_id(0) == 0)
    def _():
        big[...], low[...] = split(basis[...] * (scale * -factor))

    rb, rl = split(right[...])
    update = mm(big[...], rb, ((1,), (0,))) + mm(big[...], rl, ((1,), (0,))) + mm(low[...], rb, ((1,), (0,)))
    out[...] = weights[...].astype(f32) * (1.0 - step_rate * weight_decay) + update
    factor_out[...] = right[...].T * scale


def momentum_kernel(ids, own, other, first, second, basis, right, base, out, small):
    @pl.when(pl.program_id(0) == 0)
    def _():
        small[...] = (basis[...] * -(1.0 - mix_rate)).astype(bf16)

    total = base[...] + crossed(ids[2], own, other, first, second, 1)
    out[...] = total + mm(small[...], right[...].astype(bf16), ((1,), (0,)))


def swap(x, axis, bit):
    size = lax.axis_size(axis)
    return lax.ppermute(x, axis, [(i, i ^ bit) for i in range(size)])


def plane(n_total, m_total, inputs, out_grads, weights, momentum, right_factor):
    return plane_body(n_total, m_total, inputs, out_grads, weights, momentum, right_factor)


def swaps(x, axis, unit):
    return [swap(x, axis, unit * k) for k in (1, 2, 3)]


def plane_body(n_total, m_total, inputs, out_grads, weights, momentum, right_factor):
    rank = right_factor.shape[1]
    row = lax.axis_index("row")
    col = lax.axis_index("col")
    core, z = col % 2, col // 2
    ids = jnp.stack([row, z, core, row ^ z]).astype(jnp.int32)
    tokens, n = inputs.shape
    m = momentum.shape[0]
    block = out_grads.shape[0]
    tn = tile_of(n)
    tiles = (pl.cdiv(n, tn),)

    def columns(rows):
        return pl.BlockSpec((rows, tn), lambda i, *_: (0, i))

    def fixed(*shape):
        return pl.BlockSpec(shape, lambda i, *_: (0,) * len(shape))

    def pick(j):
        return pl.BlockSpec((1, m, block), lambda i, ids: (ids[3] ^ j, 0, 0))

    grads = out_grads.T
    own = [grads] + swaps(grads, "col", 2)

    in_right = mm(inputs.astype(f32), right_factor, ((1,), (0,)), high)
    keep = lax.dynamic_slice_in_dim(in_right, core * block, block, 0)
    send = lax.dynamic_slice_in_dim(in_right, (1 - core) * block, block, 0)
    in_right = keep + swap(send, "col", 1)
    rights = [in_right] + swaps(in_right, "row", 1)
    x_all = swap(inputs, "row", 1)
    y_all = swap(inputs, "row", 2)
    other = [swap(g, "col", 1) for g in own]
    own_all = jnp.stack(own)
    other_all = jnp.stack(other)

    part = mm(momentum, right_factor, ((1,), (0,)), high)
    keep, send = call(
        sketch_kernel, (shaped((m // 2, rank)),) * 2, (ids, part, *own, *rights),
        [whole_smem] + [whole_vmem] * 9, (whole_vmem,) * 2,
        scratch=[pltpu.VMEM((4, block, rank), bf16)] * 2, flops=4 * m * 4 * block * rank, moved=8_000_000)
    mine = keep + swap(send, "col", 1)
    size = m // 8
    total = mine[:size]
    for k in (1, 2, 3):
        total = total + swap(mine[k * size : (k + 1) * size], "col", 2 * k)
    parts = [total] + swaps(total, "col", 2)
    rest = swap(jnp.concatenate(parts, axis=0), "col", 1)

    quarter = tokens // 4
    x_first, x_second = x_all[:quarter], x_all[quarter : 2 * quarter]
    y_first, y_second = y_all[2 * quarter : 3 * quarter], y_all[3 * quarter :]
    first_by_y, first_by_x = swap(x_first, "row", 2), swap(y_first, "row", 1)
    second_by_y, second_by_x = swap(x_second, "row", 2), swap(y_second, "row", 1)

    sketch, gram, toks, big_t, low_t = call(
        gram_kernel,
        (shaped((m, rank)), shaped((rank, rank)), shaped((4, block, rank)), shaped((rank, m), bf16), shaped((rank, m), bf16)),
        (ids, *parts, rest, *own), [whole_smem] + [whole_vmem] * 9, (whole_vmem,) * 5,
        scratch=[pltpu.VMEM((rank, m), f32)], flops=20 * m * rank * rank, moved=8_000_000)
    token = toks[0]
    for k in (1, 2, 3):
        token = token + swap(toks[k], "row", k)
    token_other = swap(token, "col", 1)
    gram = gram + swap(gram, "row", 1)
    gram = gram + swap(gram, "row", 2)

    n8 = rank // 8
    sides = call(
        side_kernel, (shaped((rank // 4, n)),) * 4, (big_t, low_t, momentum),
        [whole_vmem] * 2 + [columns(m)], (columns(rank // 4),) * 4, tiles,
        flops=6 * m * n * rank, moved=5 * m * n)
    top0, top1, top_send, low0, low1, low_send = call(
        token_kernel, (shaped((n8, n)), shaped((n8, n)), shaped((2 * n8, n))) * 2,
        (ids, token, token_other, inputs, *sides),
        [whole_smem] + [whole_vmem] * 2 + [columns(tokens)] + [columns(2 * n8)] * 4,
        (columns(n8), columns(n8), columns(2 * n8)) * 2, tiles,
        scratch=[pltpu.VMEM((rank, block), f32), pltpu.VMEM((2, 2, rank, block), bf16)],
        flops=4 * tokens * n * rank, moved=10 * rank * n)
    top_in, low_in = swap(top_send, "row", 1), swap(low_send, "row", 2)
    top1, low1 = top1 + top_in[n8:], low1 + low_in[n8:]
    top0 = top0 + top_in[:n8] + swap(top1, "row", 2)
    low0 = low0 + low_in[:n8] + swap(low1, "row", 1)
    top1, low1 = swap(top0, "row", 2), swap(low0, "row", 1)
    top2 = swap(jnp.concatenate([top0, top1], axis=0), "row", 1)
    low2 = swap(jnp.concatenate([low0, low1], axis=0), "row", 2)

    inverse = inverse_factor(gram)

    def gradient(picks, crossing, blocks, base):
        count = len(picks)
        return call(
            functools.partial(gradient_kernel, count, crossing), shaped((m, n)),
            (ids, *([own_all] * count), *([other_all] * count), *blocks, base),
            [pick(j) for j in picks] * 2 + [columns(x.shape[0]) for x in blocks] + [columns(m)], columns(m), tiles,
            flops=2 * m * n * sum(x.shape[0] for x in blocks), moved=8 * m * n, prefetch=1)

    moment = gradient((0, 1), 0, (inputs, x_all), momentum)
    moment = gradient((2, 3), 1, (y_all, first_by_y, first_by_x), moment)

    right, squares, basis = call(
        functools.partial(right_kernel, n), (shaped((rank, n)), shaped((8, rank)), shaped((m, rank))),
        (ids, inverse, sketch, top0, top1, top2, low0, low1, low2),
        [whole_smem] + [whole_vmem] * 2 + [columns(n8), columns(n8), columns(2 * n8)] * 2,
        (columns(rank), fixed(8, rank), fixed(m, rank)), tiles,
        scratch=[pltpu.VMEM((rank, tn), f32)], flops=6 * n * rank * rank, moved=12 * n * rank)
    squares = squares + swap(squares, "col", 1)
    w1, w2, w3 = swaps(squares, "col", 2)
    squares = (squares + w1) + (w2 + w3)
    weights_new, factor_new = call(
        functools.partial(weights_kernel, n_total, step_rate * math.sqrt(m_total / rank)),
        (shaped((m, n)), shaped((n, rank))), (squares, basis, right, weights),
        [whole_vmem] * 2 + [columns(rank), columns(m)],
        (columns(m), pl.BlockSpec((tn, rank), lambda i, *_: (i, 0))), tiles,
        scratch=[pltpu.VMEM((m, rank), bf16)] * 2, flops=6 * m * n * rank, moved=6 * m * n)
    momentum_new = call(
        momentum_kernel, shaped((m, n)), (ids, own_all, other_all, second_by_y, second_by_x, basis, right, moment),
        [pick(3), pick(3), columns(quarter), columns(quarter), fixed(m, rank), columns(rank), columns(m)],
        columns(m), tiles, scratch=[pltpu.VMEM((m, rank), bf16)],
        flops=2 * m * n * (tokens // 2 + rank), moved=8 * m * n, prefetch=1, aliases={7: 0})
    return (weights_new, momentum_new, factor_new)


def solution(mesh):
    n_row, n_col = mesh.shape["row"], mesh.shape["col"]
    fast = (n_row, n_col) == (4, 8)
    body = plane if fast else general

    def whole(inputs, out_grads, weights, momentum, right_factor):
        m_total, n_total = weights.shape
        return jax.shard_map(
            functools.partial(body, n_total, m_total),
            mesh=mesh,
            in_specs=(P("row", "col"), P("col", "row"), P("row", "col"), P("row", "col"), P("col", None)),
            out_specs=(P("row", "col"), P("row", "col"), P("col", None)),
            check_vma=False,
        )(inputs, out_grads, weights, momentum, right_factor)

    return whole
```

```python
import functools
import math

import jax
import jax.numpy as jnp
from jax import lax
from jax.experimental import pallas as pl
from jax.experimental.pallas import tpu as pltpu
from jax.sharding import PartitionSpec as P


mix_rate = 0.95
step_rate = 0.3
weight_decay = 0.1
tiny_eps = 1e-06
highest = lax.Precision.HIGHEST
high = lax.Precision.HIGH
f32 = jnp.float32


def mm(a, b, dims, precision=None):
    return lax.dot_general(a, b, (dims, ((), ())), precision=precision, preferred_element_type=f32)


def general(n_total, m_total, inputs, out_grads, weights, momentum, right_factor):
    rank = right_factor.shape[1]
    grads_all = lax.all_gather(out_grads, "col", axis=0, tiled=True)
    inputs_all = lax.all_gather(inputs, "row", axis=0, tiled=True)
    moment = momentum + mm(grads_all, inputs_all, ((0,), (0,)))
    sketch = lax.psum(mm(moment, right_factor, ((1,), (0,)), highest), "col")
    gram = lax.psum(mm(sketch, sketch, ((0,), (0,)), highest), "row")
    inverse = inverse_factor(gram)
    basis = mm(sketch, inverse, ((1,), (1,)), highest)
    right_side = lax.psum(mm(moment, basis, ((0,), (0,)), highest), "row")
    squares = lax.psum(jnp.sum(right_side * right_side, axis=0), "col")
    factor_new = right_side * lax.rsqrt(squares / n_total + tiny_eps)
    momentum_new = moment - (1.0 - mix_rate) * mm(basis, right_side, ((1,), (1,)), highest)
    update = mm(basis, factor_new, ((1,), (1,)), highest)
    weights_new = (
        weights.astype(f32) * (1.0 - step_rate * weight_decay)
        - step_rate * math.sqrt(m_total / rank) * update
    )
    return (weights_new, momentum_new, factor_new)


def base_inverse(a):
    n = a.shape[0]
    rows = lax.broadcasted_iota(jnp.int32, (n, n), 0)
    cols = lax.broadcasted_iota(jnp.int32, (n, n), 1)
    left = a
    right = jnp.where(rows == cols, 1.0, 0.0).astype(f32)
    pivots = jnp.ones((n, n), f32)
    step = 8
    for start in range(0, n, step):
        columns = [jnp.broadcast_to(left[:, start + i : start + i + 1], (n, n)) for i in range(step)]
        for i in range(step):
            j = start + i
            pivot = jnp.broadcast_to(columns[i][j : j + 1, :], (n, n))
            pivots = jnp.where(rows == j, pivot, pivots)
            if j + 1 == n:
                break
            ratio = jnp.where(rows > j, columns[i] * (1.0 / pivot), 0.0)
            for k in range(i + 1, step):
                columns[k] = columns[k] - ratio * jnp.broadcast_to(columns[k][j : j + 1, :], (n, n))
            left = left - ratio * jnp.broadcast_to(left[j : j + 1, :], (n, n))
            right = right - ratio * jnp.broadcast_to(right[j : j + 1, :], (n, n))
    root = lax.rsqrt(pivots)
    return right * (root * (1.5 - 0.5 * pivots * root * root))


def inverse_kernel(gram_ref, out_ref, work_ref):
    n = gram_ref.shape[0]
    work_ref[...] = gram_ref[...]
    out_ref[...] = jnp.zeros_like(out_ref)

    def solve(at, size):
        span = slice(at, at + size)
        if size <= 32:
            out_ref[span, span] = base_inverse(work_ref[span, span])
            return
        half = size // 2
        one, two = slice(at, at + half), slice(at + half, at + size)
        solve(at, half)
        inv_one = out_ref[one, one]
        low = mm(work_ref[two, one], inv_one, ((1,), (1,)), highest)
        work_ref[two, two] = work_ref[two, two] - mm(low, low, ((1,), (1,)), highest)
        side = mm(low, inv_one, ((1,), (0,)), highest)
        solve(at + half, half)
        out_ref[two, one] = -mm(out_ref[two, two], side, ((1,), (0,)), highest)

    solve(0, n)


def inverse_factor(gram):
    return pl.pallas_call(
        inverse_kernel,
        out_shape=jax.ShapeDtypeStruct(gram.shape, f32),
        in_specs=[pl.BlockSpec(memory_space=pltpu.VMEM)],
        out_specs=pl.BlockSpec(memory_space=pltpu.VMEM),
        scratch_shapes=[pltpu.VMEM(gram.shape, f32)],
        cost_estimate=pl.CostEstimate(flops=20_000_000_000, bytes_accessed=10_000_000, transcendentals=0),
    )(gram)


bf16 = jnp.bfloat16
VMEM_MIB = 40
whole_vmem = pl.BlockSpec(memory_space=pltpu.VMEM)
whole_smem = pl.BlockSpec(memory_space=pltpu.SMEM)


def split(x):
    big = x.astype(bf16)
    return big, (x - big.astype(f32)).astype(bf16)


def tile_of(n):
    return min(n, 512)


def call(kernel, outs, ins, specs, out_specs, grid=(), scratch=(), flops=0, moved=0, aliases={}, prefetch=0):
    return pl.pallas_call(
        kernel,
        out_shape=outs,
        grid_spec=pltpu.PrefetchScalarGridSpec(
            num_scalar_prefetch=prefetch, grid=grid, in_specs=specs, out_specs=out_specs, scratch_shapes=list(scratch)
        ),
        input_output_aliases=aliases,
        compiler_params=pltpu.CompilerParams(vmem_limit_bytes=VMEM_MIB * 2**20),
        cost_estimate=pl.CostEstimate(flops=flops, bytes_accessed=moved, transcendentals=0),
    )(*ins)


def shaped(shape, dtype=f32):
    return jax.ShapeDtypeStruct(shape, dtype)


def sketch_kernel(ids, part, *refs):
    grads, rights, keep, send, big, low = refs[:4], refs[4:8], refs[8], refs[9], refs[10], refs[11]
    z, core, shift = ids[1], ids[2], ids[3]
    for k in range(4):
        big[k], low[k] = split(rights[k][...])
    rows = keep.shape[0] // 4
    for out, half in ((keep, core), (send, 1 - core)):
        for b in range(4):
            at = pl.ds(pl.multiple_of(half * (4 * rows) + (z ^ b) * rows, 32), rows)
            total = part[at, :]
            for k in range(4):
                g = grads[k][at, :]
                total += mm(g, big[k ^ shift], ((1,), (0,)))
                total += mm(g, low[k ^ shift], ((1,), (0,)))
            out[b * rows : (b + 1) * rows, :] = total


def gram_kernel(ids, *refs):
    parts, other, grads = refs[:4], refs[4], refs[5:9]
    sketch, gram, t0, t1, t2, t3, big_t, low_t, flip, tokens = refs[9:]
    row, z, core, shift = ids[0], ids[1], ids[2], ids[3]
    rows = parts[0].shape[0]
    for k in range(4):
        at = pl.multiple_of((z ^ k) * rows, 32)
        sketch[pl.ds(core * (4 * rows) + at, rows), :] = parts[k][...]
        sketch[pl.ds((1 - core) * (4 * rows) + at, rows), :] = other[k * rows : (k + 1) * rows, :]
    s = sketch[...]
    gram[...] = mm(s, s, ((0,), (0,)), highest)
    big, low = split(s)
    for k in range(4):
        g = grads[k][...]
        tokens[k ^ shift] = mm(g, big, ((0,), (0,))) + mm(g, low, ((0,), (0,)))
    for j, ref in enumerate((t0, t1, t2, t3)):
        ref[...] = tokens[j]
    flip[...] = s.T
    size = flip.shape[0] // 8
    for i in range(8):
        at = pl.multiple_of(rank_block(row, i) * size, 32)
        b, l = split(flip[pl.ds(at, size), :])
        big_t[i * size : (i + 1) * size, :] = b
        low_t[i * size : (i + 1) * size, :] = l


def rank_block(row, i):
    bit_x, bit_y = row % 2, row // 2
    upper, lower = (i // 2) % 2, i % 2
    if i < 4:
        return 2 * (upper ^ bit_x) + (lower ^ bit_y)
    return 4 + 2 * (upper ^ bit_y) + (lower ^ bit_x)


def side_kernel(big_t, low_t, momentum, top_keep, top_send, low_keep, low_send):
    mb, ml = split(momentum[...])
    total = mm(big_t[...], mb, ((1,), (0,)))
    total += mm(big_t[...], ml, ((1,), (0,)))
    total += mm(low_t[...], mb, ((1,), (0,)))
    n = top_keep.shape[0]
    for i, ref in enumerate((top_keep, top_send, low_keep, low_send)):
        ref[...] = total[i * n : (i + 1) * n, :]


def token_kernel(ids, own, other, inputs, *refs):
    before, after_refs, flip, tok = refs[:4], refs[4:10], refs[10], refs[11]
    row, core = ids[0], ids[2]
    half = own.shape[0]
    size = flip.shape[0] // 8

    @pl.when(pl.program_id(0) == 0)
    def _():
        for ref, place in ((own, core), (other, 1 - core)):
            flip[...] = ref[...].T
            for i in range(8):
                at = pl.multiple_of(rank_block(row, i) * size, 32)
                b, l = split(flip[pl.ds(at, size), :])
                tok[place, 0, i * size : (i + 1) * size, :] = b
                tok[place, 1, i * size : (i + 1) * size, :] = l

    total = 0.0
    for h in range(2):
        x = inputs[h * half : (h + 1) * half, :]
        total += mm(tok[h, 0], x, ((1,), (0,)))
        total += mm(tok[h, 1], x, ((1,), (0,)))
    for p in range(2):
        keep, send = before[2 * p], before[2 * p + 1]
        first, second, out = after_refs[3 * p : 3 * p + 3]
        at = 4 * p * size
        first[...] = keep[:size, :] + total[at : at + size, :]
        second[...] = keep[size:, :] + total[at + size : at + 2 * size, :]
        out[...] = send[...] + total[at + 2 * size : at + 4 * size, :]


def gradient_kernel(numbers, ids, *refs):
    count = len(numbers) // 2
    own, other, pieces = refs[:count], refs[count : 2 * count], list(refs[2 * count : -2])
    base, out = refs[-2], refs[-1]
    total = base[...]
    for at, number in enumerate(numbers):
        x = jnp.concatenate([pieces.pop(0)[...] for _ in range(number)], axis=0)
        grad = jnp.where(ids[2] == at % 2, own[at // 2][0], other[at // 2][0])
        total += mm(grad, x, ((1,), (0,)))
    out[...] = total


def right_kernel(n, ids, inverse, sketch, *refs):
    pieces, right, squares, basis, work = refs[:6], refs[6], refs[7], refs[8], refs[9]
    row = ids[0]
    size = work.shape[0] // 8

    @pl.when(pl.program_id(0) == 0)
    def _():
        sb, sl = split(sketch[...])
        ib, il = split(inverse[...])
        basis[...] = mm(sb, ib, ((1,), (1,))) + mm(sb, il, ((1,), (1,))) + mm(sl, ib, ((1,), (1,)))
        squares[...] = jnp.zeros_like(squares)

    place = 0
    for ref in pieces:
        for i in range(ref.shape[0] // size):
            at = pl.multiple_of(rank_block(row, place) * size, 32)
            work[pl.ds(at, size), :] = ref[i * size : (i + 1) * size, :]
            place += 1
    ib, il = split(inverse[...])
    tb, tl = split(work[...])
    total = mm(ib, tb, ((1,), (0,))) + mm(ib, tl, ((1,), (0,))) + mm(il, tb, ((1,), (0,)))
    right[...] = total
    at = pl.program_id(0) * total.shape[1] + lax.broadcasted_iota(jnp.int32, total.shape, 1)
    sb, sl = split(jnp.where(at < n, total * total, 0.0))
    ones = jnp.ones((8, total.shape[1]), bf16)
    squares[...] += mm(ones, sb, ((1,), (1,))) + mm(ones, sl, ((1,), (1,)))


def weights_kernel(n_total, factor, squares, basis, right, weights, out, factor_out, big, low):
    scale = lax.rsqrt(squares[0:1, :] / n_total + tiny_eps)

    @pl.when(pl.program_id(0) == 0)
    def _():
        big[...], low[...] = split(basis[...] * (scale * -factor))

    rb, rl = split(right[...])
    update = mm(big[...], rb, ((1,), (0,))) + mm(big[...], rl, ((1,), (0,))) + mm(low[...], rb, ((1,), (0,)))
    out[...] = weights[...].astype(f32) * (1.0 - step_rate * weight_decay) + update
    factor_out[...] = right[...].T * scale


def momentum_kernel(basis, right, base, out, small):
    @pl.when(pl.program_id(0) == 0)
    def _():
        small[...] = (basis[...] * -(1.0 - mix_rate)).astype(bf16)

    out[...] = base[...] + mm(small[...], right[...].astype(bf16), ((1,), (0,)))


def swap(x, axis, bit):
    size = lax.axis_size(axis)
    return lax.ppermute(x, axis, [(i, i ^ bit) for i in range(size)])


def plane(n_total, m_total, inputs, out_grads, weights, momentum, right_factor):
    return plane_body(n_total, m_total, inputs, out_grads, weights, momentum, right_factor)


def swaps(x, axis, unit):
    return [swap(x, axis, unit * k) for k in (1, 2, 3)]


def plane_body(n_total, m_total, inputs, out_grads, weights, momentum, right_factor):
    rank = right_factor.shape[1]
    row = lax.axis_index("row")
    col = lax.axis_index("col")
    core, z = col % 2, col // 2
    ids = jnp.stack([row, z, core, row ^ z]).astype(jnp.int32)
    tokens, n = inputs.shape
    m = momentum.shape[0]
    block = out_grads.shape[0]
    tn = tile_of(n)
    tiles = (pl.cdiv(n, tn),)

    def columns(rows):
        return pl.BlockSpec((rows, tn), lambda i, *_: (0, i))

    def fixed(*shape):
        return pl.BlockSpec(shape, lambda i, *_: (0,) * len(shape))

    def pick(j):
        return pl.BlockSpec((1, m, block), lambda i, ids: (ids[3] ^ j, 0, 0))

    grads = out_grads.T
    own = [grads] + swaps(grads, "col", 2)

    in_right = mm(inputs.astype(f32), right_factor, ((1,), (0,)), high)
    keep = lax.dynamic_slice_in_dim(in_right, core * block, block, 0)
    send = lax.dynamic_slice_in_dim(in_right, (1 - core) * block, block, 0)
    in_right = keep + swap(send, "col", 1)
    rights = [in_right] + swaps(in_right, "row", 1)
    quarter = tokens // 4
    cut0, cut2 = inputs[:quarter], inputs[2 * quarter : 3 * quarter]
    cut1, cut3 = inputs[quarter : 2 * quarter], inputs[3 * quarter :]
    half0, half1 = inputs[: 2 * quarter], inputs[2 * quarter :]
    x0, y2 = swap(cut0, "row", 1), swap(cut2, "row", 2)
    x1, y3 = swap(cut1, "row", 1), swap(cut3, "row", 2)
    x23, y01 = swap(half1, "row", 1), swap(half0, "row", 2)
    other = [swap(g, "col", 1) for g in own]
    own_all = jnp.stack(own)
    other_all = jnp.stack(other)

    part = mm(momentum, right_factor, ((1,), (0,)), high)
    keep, send = call(
        sketch_kernel, (shaped((m // 2, rank)),) * 2, (ids, part, *own, *rights),
        [whole_smem] + [whole_vmem] * 9, (whole_vmem,) * 2,
        scratch=[pltpu.VMEM((4, block, rank), bf16)] * 2, flops=4 * m * 4 * block * rank, moved=8_000_000)
    mine = keep + swap(send, "col", 1)
    size = m // 8
    total = mine[:size]
    for k in (1, 2, 3):
        total = total + swap(mine[k * size : (k + 1) * size], "col", 2 * k)
    parts = [total] + swaps(total, "col", 2)
    rest = swap(jnp.concatenate(parts, axis=0), "col", 1)

    first_by_y, first_by_x = swap(x0, "row", 2), swap(y2, "row", 1)
    second_by_y, second_by_x = swap(x1, "row", 2), swap(y3, "row", 1)

    sketch, gram, *toks, big_t, low_t = call(
        gram_kernel,
        (shaped((m, rank)), shaped((rank, rank)), *([shaped((block, rank))] * 4), shaped((rank, m), bf16), shaped((rank, m), bf16)),
        (ids, *parts, rest, *own), [whole_smem] + [whole_vmem] * 9, (whole_vmem,) * 8,
        scratch=[pltpu.VMEM((rank, m), f32), pltpu.VMEM((4, block, rank), f32)], flops=20 * m * rank * rank, moved=8_000_000)
    token = toks[0]
    for k in (1, 2, 3):
        token = token + swap(toks[k], "row", k)
    token_other = swap(token, "col", 1)
    gram = gram + swap(gram, "row", 1)
    gram = gram + swap(gram, "row", 2)

    n8 = rank // 8
    sides = call(
        side_kernel, (shaped((rank // 4, n)),) * 4, (big_t, low_t, momentum),
        [whole_vmem] * 2 + [columns(m)], (columns(rank // 4),) * 4, tiles,
        flops=6 * m * n * rank, moved=5 * m * n)
    top0, top1, top_send, low0, low1, low_send = call(
        token_kernel, (shaped((n8, n)), shaped((n8, n)), shaped((2 * n8, n))) * 2,
        (ids, token, token_other, inputs, *sides),
        [whole_smem] + [whole_vmem] * 2 + [columns(tokens)] + [columns(2 * n8)] * 4,
        (columns(n8), columns(n8), columns(2 * n8)) * 2, tiles,
        scratch=[pltpu.VMEM((rank, block), f32), pltpu.VMEM((2, 2, rank, block), bf16)],
        flops=4 * tokens * n * rank, moved=10 * rank * n)
    top_in, low_in = swap(top_send, "row", 1), swap(low_send, "row", 2)
    top1, low1 = top1 + top_in[n8:], low1 + low_in[n8:]
    top0 = top0 + top_in[:n8] + swap(top1, "row", 2)
    low0 = low0 + low_in[:n8] + swap(low1, "row", 1)
    top1, low1 = swap(top0, "row", 2), swap(low0, "row", 1)
    top2 = swap(jnp.concatenate([top0, top1], axis=0), "row", 1)
    low2 = swap(jnp.concatenate([low0, low1], axis=0), "row", 2)

    inverse = inverse_factor(gram)

    def gradient(picks, numbers, pieces, base):
        return call(
            functools.partial(gradient_kernel, numbers), shaped((m, n)),
            (ids, *([own_all] * len(picks)), *([other_all] * len(picks)), *pieces, base),
            [pick(j) for j in picks] * 2 + [columns(x.shape[0]) for x in pieces] + [columns(m)], columns(m), tiles,
            flops=2 * m * n * sum(x.shape[0] for x in pieces), moved=8 * m * n, prefetch=1)

    moment = gradient((0, 1), (1, 1, 2, 1), (half0, half1, x0, x1, x23), momentum)
    moment = gradient(
        (2, 3), (1, 2, 2, 2), (y01, y2, y3, first_by_y, second_by_y, first_by_x, second_by_x), moment)

    right, squares, basis = call(
        functools.partial(right_kernel, n), (shaped((rank, n)), shaped((8, rank)), shaped((m, rank))),
        (ids, inverse, sketch, top0, top1, top2, low0, low1, low2),
        [whole_smem] + [whole_vmem] * 2 + [columns(n8), columns(n8), columns(2 * n8)] * 2,
        (columns(rank), fixed(8, rank), fixed(m, rank)), tiles,
        scratch=[pltpu.VMEM((rank, tn), f32)], flops=6 * n * rank * rank, moved=12 * n * rank)
    squares = squares + swap(squares, "col", 1)
    w1, w2, w3 = swaps(squares, "col", 2)
    squares = (squares + w1) + (w2 + w3)
    weights_new, factor_new = call(
        functools.partial(weights_kernel, n_total, step_rate * math.sqrt(m_total / rank)),
        (shaped((m, n)), shaped((n, rank))), (squares, basis, right, weights),
        [whole_vmem] * 2 + [columns(rank), columns(m)],
        (columns(m), pl.BlockSpec((tn, rank), lambda i, *_: (i, 0))), tiles,
        scratch=[pltpu.VMEM((m, rank), bf16)] * 2, flops=6 * m * n * rank, moved=6 * m * n)
    momentum_new = call(
        momentum_kernel, shaped((m, n)), (basis, right, moment), [fixed(m, rank), columns(rank), columns(m)],
        columns(m), tiles, scratch=[pltpu.VMEM((m, rank), bf16)],
        flops=2 * m * n * rank, moved=8 * m * n, aliases={2: 0})
    return (weights_new, momentum_new, factor_new)


def solution(mesh):
    n_row, n_col = mesh.shape["row"], mesh.shape["col"]
    fast = (n_row, n_col) == (4, 8)
    body = plane if fast else general

    def whole(inputs, out_grads, weights, momentum, right_factor):
        m_total, n_total = weights.shape
        return jax.shard_map(
            functools.partial(body, n_total, m_total),
            mesh=mesh,
            in_specs=(P("row", "col"), P("col", "row"), P("row", "col"), P("row", "col"), P("col", None)),
            out_specs=(P("row", "col"), P("row", "col"), P("col", None)),
            check_vma=False,
        )(inputs, out_grads, weights, momentum, right_factor)

    return whole
```

```python
import functools
import math

import jax
import jax.numpy as jnp
from jax import lax
from jax.experimental import pallas as pl
from jax.experimental.pallas import tpu as pltpu
from jax.sharding import PartitionSpec as P


mix_rate = 0.95
step_rate = 0.3
weight_decay = 0.1
tiny_eps = 1e-06
highest = lax.Precision.HIGHEST
high = lax.Precision.HIGH
f32 = jnp.float32


def mm(a, b, dims, precision=None):
    return lax.dot_general(a, b, (dims, ((), ())), precision=precision, preferred_element_type=f32)


def general(n_total, m_total, inputs, out_grads, weights, momentum, right_factor):
    rank = right_factor.shape[1]
    grads_all = lax.all_gather(out_grads, "col", axis=0, tiled=True)
    inputs_all = lax.all_gather(inputs, "row", axis=0, tiled=True)
    moment = momentum + mm(grads_all, inputs_all, ((0,), (0,)))
    sketch = lax.psum(mm(moment, right_factor, ((1,), (0,)), highest), "col")
    gram = lax.psum(mm(sketch, sketch, ((0,), (0,)), highest), "row")
    inverse = inverse_factor(gram)
    basis = mm(sketch, inverse, ((1,), (1,)), highest)
    right_side = lax.psum(mm(moment, basis, ((0,), (0,)), highest), "row")
    squares = lax.psum(jnp.sum(right_side * right_side, axis=0), "col")
    factor_new = right_side * lax.rsqrt(squares / n_total + tiny_eps)
    momentum_new = moment - (1.0 - mix_rate) * mm(basis, right_side, ((1,), (1,)), highest)
    update = mm(basis, factor_new, ((1,), (1,)), highest)
    weights_new = (
        weights.astype(f32) * (1.0 - step_rate * weight_decay)
        - step_rate * math.sqrt(m_total / rank) * update
    )
    return (weights_new, momentum_new, factor_new)


def base_inverse(a):
    n = a.shape[0]
    rows = lax.broadcasted_iota(jnp.int32, (n, n), 0)
    cols = lax.broadcasted_iota(jnp.int32, (n, n), 1)
    left = a
    right = jnp.where(rows == cols, 1.0, 0.0).astype(f32)
    pivots = jnp.ones((n, n), f32)
    step = 8
    for start in range(0, n, step):
        columns = [jnp.broadcast_to(left[:, start + i : start + i + 1], (n, n)) for i in range(step)]
        for i in range(step):
            j = start + i
            pivot = jnp.broadcast_to(columns[i][j : j + 1, :], (n, n))
            pivots = jnp.where(rows == j, pivot, pivots)
            if j + 1 == n:
                break
            ratio = jnp.where(rows > j, columns[i] * (1.0 / pivot), 0.0)
            for k in range(i + 1, step):
                columns[k] = columns[k] - ratio * jnp.broadcast_to(columns[k][j : j + 1, :], (n, n))
            left = left - ratio * jnp.broadcast_to(left[j : j + 1, :], (n, n))
            right = right - ratio * jnp.broadcast_to(right[j : j + 1, :], (n, n))
    root = lax.rsqrt(pivots)
    return right * (root * (1.5 - 0.5 * pivots * root * root))


def inverse_kernel(gram_ref, out_ref, work_ref):
    n = gram_ref.shape[0]
    work_ref[...] = gram_ref[...]
    out_ref[...] = jnp.zeros_like(out_ref)

    def solve(at, size):
        span = slice(at, at + size)
        if size <= 32:
            out_ref[span, span] = base_inverse(work_ref[span, span])
            return
        half = size // 2
        one, two = slice(at, at + half), slice(at + half, at + size)
        solve(at, half)
        inv_one = out_ref[one, one]
        low = mm(work_ref[two, one], inv_one, ((1,), (1,)), highest)
        work_ref[two, two] = work_ref[two, two] - mm(low, low, ((1,), (1,)), highest)
        side = mm(low, inv_one, ((1,), (0,)), highest)
        solve(at + half, half)
        out_ref[two, one] = -mm(out_ref[two, two], side, ((1,), (0,)), highest)

    solve(0, n)


def inverse_factor(gram):
    return pl.pallas_call(
        inverse_kernel,
        out_shape=jax.ShapeDtypeStruct(gram.shape, f32),
        in_specs=[pl.BlockSpec(memory_space=pltpu.VMEM)],
        out_specs=pl.BlockSpec(memory_space=pltpu.VMEM),
        scratch_shapes=[pltpu.VMEM(gram.shape, f32)],
        cost_estimate=pl.CostEstimate(flops=20_000_000_000, bytes_accessed=10_000_000, transcendentals=0),
    )(gram)


bf16 = jnp.bfloat16
VMEM_MIB = 40
whole_vmem = pl.BlockSpec(memory_space=pltpu.VMEM)
whole_smem = pl.BlockSpec(memory_space=pltpu.SMEM)


def split(x):
    big = x.astype(bf16)
    return big, (x - big.astype(f32)).astype(bf16)


def tile_of(n):
    return min(n, 512)


def call(kernel, outs, ins, specs, out_specs, grid=(), scratch=(), flops=0, moved=0, aliases={}, prefetch=0):
    return pl.pallas_call(
        kernel,
        out_shape=outs,
        grid_spec=pltpu.PrefetchScalarGridSpec(
            num_scalar_prefetch=prefetch, grid=grid, in_specs=specs, out_specs=out_specs, scratch_shapes=list(scratch)
        ),
        input_output_aliases=aliases,
        compiler_params=pltpu.CompilerParams(vmem_limit_bytes=VMEM_MIB * 2**20),
        cost_estimate=pl.CostEstimate(flops=flops, bytes_accessed=moved, transcendentals=0),
    )(*ins)


def shaped(shape, dtype=f32):
    return jax.ShapeDtypeStruct(shape, dtype)


def sketch_kernel(ids, part, *refs):
    grads, rights, keep, send, big, low = refs[:6], refs[6:10], refs[10], refs[11], refs[12], refs[13]
    z, core, shift = ids[1], ids[2], ids[3]
    for k in range(4):
        big[k], low[k] = split(rights[k][...])
    rows = keep.shape[0] // 4
    for out, half in ((keep, core), (send, 1 - core)):
        for b in range(4):
            at = pl.ds(pl.multiple_of(half * (4 * rows) + (z ^ b) * rows, 32), rows)
            total = part[at, :]
            for k, grad in zip((0, 1, 3, 2, 2, 3), grads):
                g = grad[at, :]
                total += mm(g, big[k ^ shift], ((1,), (0,)))
                total += mm(g, low[k ^ shift], ((1,), (0,)))
            out[b * rows : (b + 1) * rows, :] = total


def gram_kernel(ids, *refs):
    parts, other, grads = refs[:4], refs[4], refs[5:9]
    sketch, gram, t0, t1, t2, t3, big_t, low_t, flip, tokens = refs[9:]
    row, z, core, shift = ids[0], ids[1], ids[2], ids[3]
    rows = parts[0].shape[0]
    for k in range(4):
        at = pl.multiple_of((z ^ k) * rows, 32)
        sketch[pl.ds(core * (4 * rows) + at, rows), :] = parts[k][...]
        sketch[pl.ds((1 - core) * (4 * rows) + at, rows), :] = other[k * rows : (k + 1) * rows, :]
    s = sketch[...]
    gram[...] = mm(s, s, ((0,), (0,)), highest)
    big, low = split(s)
    for k in range(4):
        g = grads[k][...]
        tokens[k ^ shift] = mm(g, big, ((0,), (0,))) + mm(g, low, ((0,), (0,)))
    for j, ref in enumerate((t0, t1, t2, t3)):
        ref[...] = tokens[j]
    flip[...] = s.T
    size = flip.shape[0] // 8
    for i in range(8):
        at = pl.multiple_of(rank_block(row, i) * size, 32)
        b, l = split(flip[pl.ds(at, size), :])
        big_t[i * size : (i + 1) * size, :] = b
        low_t[i * size : (i + 1) * size, :] = l


def rank_block(row, i):
    bit_x, bit_y = row % 2, row // 2
    upper, lower = (i // 2) % 2, i % 2
    if i < 4:
        return 2 * (upper ^ bit_x) + (lower ^ bit_y)
    return 4 + 2 * (upper ^ bit_y) + (lower ^ bit_x)


def side_kernel(big_t, low_t, momentum, top_keep, top_send, low_keep, low_send):
    mb, ml = split(momentum[...])
    total = mm(big_t[...], mb, ((1,), (0,)))
    total += mm(big_t[...], ml, ((1,), (0,)))
    total += mm(low_t[...], mb, ((1,), (0,)))
    n = top_keep.shape[0]
    for i, ref in enumerate((top_keep, top_send, low_keep, low_send)):
        ref[...] = total[i * n : (i + 1) * n, :]


def token_kernel(ids, own, other, inputs, *refs):
    before, after_refs, flip, tok = refs[:4], refs[4:10], refs[10], refs[11]
    row, core = ids[0], ids[2]
    half = own.shape[0]
    size = flip.shape[0] // 8

    @pl.when(pl.program_id(0) == 0)
    def _():
        for ref, place in ((own, core), (other, 1 - core)):
            flip[...] = ref[...].T
            for i in range(8):
                at = pl.multiple_of(rank_block(row, i) * size, 32)
                b, l = split(flip[pl.ds(at, size), :])
                tok[place, 0, i * size : (i + 1) * size, :] = b
                tok[place, 1, i * size : (i + 1) * size, :] = l

    total = 0.0
    for h in range(2):
        x = inputs[h * half : (h + 1) * half, :]
        total += mm(tok[h, 0], x, ((1,), (0,)))
        total += mm(tok[h, 1], x, ((1,), (0,)))
    for p in range(2):
        keep, send = before[2 * p], before[2 * p + 1]
        first, second, out = after_refs[3 * p : 3 * p + 3]
        at = 4 * p * size
        first[...] = keep[:size, :] + total[at : at + size, :]
        second[...] = keep[size:, :] + total[at + size : at + 2 * size, :]
        out[...] = send[...] + total[at + 2 * size : at + 4 * size, :]


def gradient_kernel(numbers, cuts, ids, *refs):
    count = len(numbers) // 2
    own, other, pieces = refs[:count], refs[count : 2 * count], list(refs[2 * count : -2])
    base, out = refs[-2], refs[-1]
    total = base[...]
    for at, number in enumerate(numbers):
        x = jnp.concatenate([pieces.pop(0)[...] for _ in range(number)], axis=0)
        cut = cuts[at // 2]
        grad = jnp.where(ids[2] == at % 2, own[at // 2][0, :, cut], other[at // 2][0, :, cut])
        total += mm(grad, x, ((1,), (0,)))
    out[...] = total


def right_kernel(n, ids, inverse, sketch, *refs):
    pieces, right, squares, basis, work = refs[:6], refs[6], refs[7], refs[8], refs[9]
    row = ids[0]
    size = work.shape[0] // 8

    @pl.when(pl.program_id(0) == 0)
    def _():
        sb, sl = split(sketch[...])
        ib, il = split(inverse[...])
        basis[...] = mm(sb, ib, ((1,), (1,))) + mm(sb, il, ((1,), (1,))) + mm(sl, ib, ((1,), (1,)))
        squares[...] = jnp.zeros_like(squares)

    place = 0
    for ref in pieces:
        for i in range(ref.shape[0] // size):
            at = pl.multiple_of(rank_block(row, place) * size, 32)
            work[pl.ds(at, size), :] = ref[i * size : (i + 1) * size, :]
            place += 1
    ib, il = split(inverse[...])
    tb, tl = split(work[...])
    total = mm(ib, tb, ((1,), (0,))) + mm(ib, tl, ((1,), (0,))) + mm(il, tb, ((1,), (0,)))
    right[...] = total
    at = pl.program_id(0) * total.shape[1] + lax.broadcasted_iota(jnp.int32, total.shape, 1)
    sb, sl = split(jnp.where(at < n, total * total, 0.0))
    ones = jnp.ones((8, total.shape[1]), bf16)
    squares[...] += mm(ones, sb, ((1,), (1,))) + mm(ones, sl, ((1,), (1,)))


def weights_kernel(n_total, factor, squares, basis, right, weights, out, factor_out, big, low):
    scale = lax.rsqrt(squares[0:1, :] / n_total + tiny_eps)

    @pl.when(pl.program_id(0) == 0)
    def _():
        big[...], low[...] = split(basis[...] * (scale * -factor))

    rb, rl = split(right[...])
    update = mm(big[...], rb, ((1,), (0,))) + mm(big[...], rl, ((1,), (0,))) + mm(low[...], rb, ((1,), (0,)))
    out[...] = weights[...].astype(f32) * (1.0 - step_rate * weight_decay) + update
    factor_out[...] = right[...].T * scale


def momentum_kernel(cut, ids, own, other, first, second, basis, right, base, out, small):
    @pl.when(pl.program_id(0) == 0)
    def _():
        small[...] = (basis[...] * -(1.0 - mix_rate)).astype(bf16)

    mine, its = own[0, :, cut], other[0, :, cut]
    total = base[...] + mm(jnp.where(ids[2] == 0, mine, its), first[...], ((1,), (0,)))
    total += mm(jnp.where(ids[2] == 0, its, mine), second[...], ((1,), (0,)))
    out[...] = total + mm(small[...], right[...].astype(bf16), ((1,), (0,)))


def swap(x, axis, bit):
    size = lax.axis_size(axis)
    return lax.ppermute(x, axis, [(i, i ^ bit) for i in range(size)])


def plane(n_total, m_total, inputs, out_grads, weights, momentum, right_factor):
    return plane_body(n_total, m_total, inputs, out_grads, weights, momentum, right_factor)


def line(x, inner):
    steps = ((1, 2), (2, 1)) if inner else ((1, 0), (2, 3))
    return lax.ppermute(x, "col", [(2 * a + h, 2 * b + h) for a, b in steps for h in range(2)])


def swaps(x, axis, unit):
    return [swap(x, axis, unit * k) for k in (1, 2, 3)]


def plane_body(n_total, m_total, inputs, out_grads, weights, momentum, right_factor):
    rank = right_factor.shape[1]
    row = lax.axis_index("row")
    col = lax.axis_index("col")
    core, z = col % 2, col // 2
    ids = jnp.stack([row, z, core, row ^ z]).astype(jnp.int32)
    tokens, n = inputs.shape
    m = momentum.shape[0]
    block = out_grads.shape[0]
    tn = tile_of(n)
    tiles = (pl.cdiv(n, tn),)

    def columns(rows):
        return pl.BlockSpec((rows, tn), lambda i, *_: (0, i))

    def fixed(*shape):
        return pl.BlockSpec(shape, lambda i, *_: (0,) * len(shape))

    def pick(j):
        return pl.BlockSpec((1, m, block), lambda i, ids: (ids[3] ^ j, 0, 0))

    grads = out_grads.T
    near = swap(grads, "col", 2)
    inner1 = line(grads, True)
    inner2 = line(near, True)
    outer1 = line(inner1, False)
    outer2 = line(inner2, False)
    own = [grads, near, inner2 + outer1, inner1 + outer2]

    in_right = mm(inputs.astype(f32), right_factor, ((1,), (0,)), high)
    keep = lax.dynamic_slice_in_dim(in_right, core * block, block, 0)
    send = lax.dynamic_slice_in_dim(in_right, (1 - core) * block, block, 0)
    in_right = keep + swap(send, "col", 1)
    rights = [in_right] + swaps(in_right, "row", 1)
    quarter = tokens // 4
    cut0, cut2 = inputs[:quarter], inputs[2 * quarter : 3 * quarter]
    cut1, cut3 = inputs[quarter : 2 * quarter], inputs[3 * quarter :]
    half0, half1 = inputs[: 2 * quarter], inputs[2 * quarter :]
    x0, y2 = swap(cut0, "row", 1), swap(cut2, "row", 2)
    x1, y3 = swap(cut1, "row", 1), swap(cut3, "row", 2)
    x23, y01 = swap(half1, "row", 1), swap(half0, "row", 2)
    other = [swap(g, "col", 1) for g in own]
    own_all = jnp.stack(own)
    other_all = jnp.stack(other)

    part = mm(momentum, right_factor, ((1,), (0,)), high)
    keep, send = call(
        sketch_kernel, (shaped((m // 2, rank)),) * 2, (ids, part, grads, near, inner1, inner2, outer1, outer2, *rights),
        [whole_smem] + [whole_vmem] * 11, (whole_vmem,) * 2,
        scratch=[pltpu.VMEM((4, block, rank), bf16)] * 2, flops=4 * m * 4 * block * rank, moved=8_000_000)
    mine = keep + swap(send, "col", 1)
    size = m // 8
    total = mine[:size]
    for k in (1, 2, 3):
        total = total + swap(mine[k * size : (k + 1) * size], "col", 2 * k)
    parts = [total] + swaps(total, "col", 2)
    rest = swap(jnp.concatenate(parts, axis=0), "col", 1)

    first_by_y, first_by_x = swap(x0, "row", 2), swap(y2, "row", 1)
    second_by_y, second_by_x = swap(x1, "row", 2), swap(y3, "row", 1)

    sketch, gram, *toks, big_t, low_t = call(
        gram_kernel,
        (shaped((m, rank)), shaped((rank, rank)), *([shaped((block, rank))] * 4), shaped((rank, m), bf16), shaped((rank, m), bf16)),
        (ids, *parts, rest, *own), [whole_smem] + [whole_vmem] * 9, (whole_vmem,) * 8,
        scratch=[pltpu.VMEM((rank, m), f32), pltpu.VMEM((4, block, rank), f32)], flops=20 * m * rank * rank, moved=8_000_000)
    token = toks[0]
    for k in (1, 2, 3):
        token = token + swap(toks[k], "row", k)
    token_other = swap(token, "col", 1)
    gram = gram + swap(gram, "row", 1)
    gram = gram + swap(gram, "row", 2)

    n8 = rank // 8
    sides = call(
        side_kernel, (shaped((rank // 4, n)),) * 4, (big_t, low_t, momentum),
        [whole_vmem] * 2 + [columns(m)], (columns(rank // 4),) * 4, tiles,
        flops=6 * m * n * rank, moved=5 * m * n)
    top0, top1, top_send, low0, low1, low_send = call(
        token_kernel, (shaped((n8, n)), shaped((n8, n)), shaped((2 * n8, n))) * 2,
        (ids, token, token_other, inputs, *sides),
        [whole_smem] + [whole_vmem] * 2 + [columns(tokens)] + [columns(2 * n8)] * 4,
        (columns(n8), columns(n8), columns(2 * n8)) * 2, tiles,
        scratch=[pltpu.VMEM((rank, block), f32), pltpu.VMEM((2, 2, rank, block), bf16)],
        flops=4 * tokens * n * rank, moved=10 * rank * n)
    top_in, low_in = swap(top_send, "row", 1), swap(low_send, "row", 2)
    top1, low1 = top1 + top_in[n8:], low1 + low_in[n8:]
    top0 = top0 + top_in[:n8] + swap(top1, "row", 2)
    low0 = low0 + low_in[:n8] + swap(low1, "row", 1)
    top1, low1 = swap(top0, "row", 2), swap(low0, "row", 1)
    top2 = swap(jnp.concatenate([top0, top1], axis=0), "row", 1)
    low2 = swap(jnp.concatenate([low0, low1], axis=0), "row", 2)

    inverse = inverse_factor(gram)

    every, early, late = slice(None), slice(0, quarter), slice(quarter, 2 * quarter)

    def gradient(picks, numbers, cuts, pieces, base):
        return call(
            functools.partial(gradient_kernel, numbers, cuts), shaped((m, n)),
            (ids, *([own_all] * len(picks)), *([other_all] * len(picks)), *pieces, base),
            [pick(j) for j in picks] * 2 + [columns(x.shape[0]) for x in pieces] + [columns(m)], columns(m), tiles,
            flops=2 * m * n * sum(x.shape[0] for x in pieces), moved=8 * m * n, prefetch=1)

    moment = gradient((0, 1), (1, 1, 2, 1), (every, every), (half0, half1, x0, x1, x23), momentum)
    moment = gradient(
        (2, 3), (1, 2, 1, 1), (every, early), (y01, y2, y3, first_by_y, first_by_x), moment)

    right, squares, basis = call(
        functools.partial(right_kernel, n), (shaped((rank, n)), shaped((8, rank)), shaped((m, rank))),
        (ids, inverse, sketch, top0, top1, top2, low0, low1, low2),
        [whole_smem] + [whole_vmem] * 2 + [columns(n8), columns(n8), columns(2 * n8)] * 2,
        (columns(rank), fixed(8, rank), fixed(m, rank)), tiles,
        scratch=[pltpu.VMEM((rank, tn), f32)], flops=6 * n * rank * rank, moved=12 * n * rank)
    squares = squares + swap(squares, "col", 1)
    w1, w2, w3 = swaps(squares, "col", 2)
    squares = (squares + w1) + (w2 + w3)
    weights_new, factor_new = call(
        functools.partial(weights_kernel, n_total, step_rate * math.sqrt(m_total / rank)),
        (shaped((m, n)), shaped((n, rank))), (squares, basis, right, weights),
        [whole_vmem] * 2 + [columns(rank), columns(m)],
        (columns(m), pl.BlockSpec((tn, rank), lambda i, *_: (i, 0))), tiles,
        scratch=[pltpu.VMEM((m, rank), bf16)] * 2, flops=6 * m * n * rank, moved=6 * m * n)
    momentum_new = call(
        functools.partial(momentum_kernel, late), shaped((m, n)),
        (ids, own_all, other_all, second_by_y, second_by_x, basis, right, moment),
        [pick(3), pick(3), columns(quarter), columns(quarter), fixed(m, rank), columns(rank), columns(m)],
        columns(m), tiles, scratch=[pltpu.VMEM((m, rank), bf16)],
        flops=2 * m * n * (tokens // 2 + rank), moved=8 * m * n, prefetch=1, aliases={7: 0})
    return (weights_new, momentum_new, factor_new)


def solution(mesh):
    n_row, n_col = mesh.shape["row"], mesh.shape["col"]
    fast = (n_row, n_col) == (4, 8)
    body = plane if fast else general

    def whole(inputs, out_grads, weights, momentum, right_factor):
        m_total, n_total = weights.shape
        return jax.shard_map(
            functools.partial(body, n_total, m_total),
            mesh=mesh,
            in_specs=(P("row", "col"), P("col", "row"), P("row", "col"), P("row", "col"), P("col", None)),
            out_specs=(P("row", "col"), P("row", "col"), P("col", None)),
            check_vma=False,
        )(inputs, out_grads, weights, momentum, right_factor)

    return whole
```

```python
import functools
import math

import jax
import jax.numpy as jnp
from jax import lax
from jax.experimental import pallas as pl
from jax.experimental.pallas import tpu as pltpu
from jax.sharding import PartitionSpec as P


mix_rate = 0.95
step_rate = 0.3
weight_decay = 0.1
tiny_eps = 1e-06
highest = lax.Precision.HIGHEST
high = lax.Precision.HIGH
f32 = jnp.float32


def mm(a, b, dims, precision=None):
    return lax.dot_general(a, b, (dims, ((), ())), precision=precision, preferred_element_type=f32)


def general(n_total, m_total, inputs, out_grads, weights, momentum, right_factor):
    rank = right_factor.shape[1]
    grads_all = lax.all_gather(out_grads, "col", axis=0, tiled=True)
    inputs_all = lax.all_gather(inputs, "row", axis=0, tiled=True)
    moment = momentum + mm(grads_all, inputs_all, ((0,), (0,)))
    sketch = lax.psum(mm(moment, right_factor, ((1,), (0,)), highest), "col")
    gram = lax.psum(mm(sketch, sketch, ((0,), (0,)), highest), "row")
    inverse = inverse_factor(gram)
    basis = mm(sketch, inverse, ((1,), (1,)), highest)
    right_side = lax.psum(mm(moment, basis, ((0,), (0,)), highest), "row")
    squares = lax.psum(jnp.sum(right_side * right_side, axis=0), "col")
    factor_new = right_side * lax.rsqrt(squares / n_total + tiny_eps)
    momentum_new = moment - (1.0 - mix_rate) * mm(basis, right_side, ((1,), (1,)), highest)
    update = mm(basis, factor_new, ((1,), (1,)), highest)
    weights_new = (
        weights.astype(f32) * (1.0 - step_rate * weight_decay)
        - step_rate * math.sqrt(m_total / rank) * update
    )
    return (weights_new, momentum_new, factor_new)


def base_inverse(a):
    n = a.shape[0]
    rows = lax.broadcasted_iota(jnp.int32, (n, n), 0)
    cols = lax.broadcasted_iota(jnp.int32, (n, n), 1)
    left = a
    right = jnp.where(rows == cols, 1.0, 0.0).astype(f32)
    pivots = jnp.ones((n, n), f32)
    step = 8
    for start in range(0, n, step):
        columns = [jnp.broadcast_to(left[:, start + i : start + i + 1], (n, n)) for i in range(step)]
        for i in range(step):
            j = start + i
            pivot = jnp.broadcast_to(columns[i][j : j + 1, :], (n, n))
            pivots = jnp.where(rows == j, pivot, pivots)
            if j + 1 == n:
                break
            ratio = jnp.where(rows > j, columns[i] * (1.0 / pivot), 0.0)
            for k in range(i + 1, step):
                columns[k] = columns[k] - ratio * jnp.broadcast_to(columns[k][j : j + 1, :], (n, n))
            left = left - ratio * jnp.broadcast_to(left[j : j + 1, :], (n, n))
            right = right - ratio * jnp.broadcast_to(right[j : j + 1, :], (n, n))
    root = lax.rsqrt(pivots)
    return right * (root * (1.5 - 0.5 * pivots * root * root))


def inverse_kernel(gram_ref, out_ref, work_ref):
    n = gram_ref.shape[0]
    work_ref[...] = gram_ref[...]
    out_ref[...] = jnp.zeros_like(out_ref)

    def solve(at, size):
        span = slice(at, at + size)
        if size <= 32:
            out_ref[span, span] = base_inverse(work_ref[span, span])
            return
        half = size // 2
        one, two = slice(at, at + half), slice(at + half, at + size)
        solve(at, half)
        inv_one = out_ref[one, one]
        low = mm(work_ref[two, one], inv_one, ((1,), (1,)), highest)
        work_ref[two, two] = work_ref[two, two] - mm(low, low, ((1,), (1,)), highest)
        side = mm(low, inv_one, ((1,), (0,)), highest)
        solve(at + half, half)
        out_ref[two, one] = -mm(out_ref[two, two], side, ((1,), (0,)), highest)

    solve(0, n)


def inverse_factor(gram):
    return pl.pallas_call(
        inverse_kernel,
        out_shape=jax.ShapeDtypeStruct(gram.shape, f32),
        in_specs=[pl.BlockSpec(memory_space=pltpu.VMEM)],
        out_specs=pl.BlockSpec(memory_space=pltpu.VMEM),
        scratch_shapes=[pltpu.VMEM(gram.shape, f32)],
        cost_estimate=pl.CostEstimate(flops=20_000_000_000, bytes_accessed=10_000_000, transcendentals=0),
    )(gram)


bf16 = jnp.bfloat16
VMEM_MIB = 30
whole_vmem = pl.BlockSpec(memory_space=pltpu.VMEM)
whole_smem = pl.BlockSpec(memory_space=pltpu.SMEM)


def split(x):
    big = x.astype(bf16)
    return big, (x - big.astype(f32)).astype(bf16)


def tile_of(n):
    return min(n, 512)


def call(kernel, outs, ins, specs, out_specs, grid=(), scratch=(), flops=0, moved=0, aliases={}, prefetch=0):
    return pl.pallas_call(
        kernel,
        out_shape=outs,
        grid_spec=pltpu.PrefetchScalarGridSpec(
            num_scalar_prefetch=prefetch, grid=grid, in_specs=specs, out_specs=out_specs, scratch_shapes=list(scratch)
        ),
        input_output_aliases=aliases,
        compiler_params=pltpu.CompilerParams(vmem_limit_bytes=VMEM_MIB * 2**20),
        cost_estimate=pl.CostEstimate(flops=flops, bytes_accessed=moved, transcendentals=0),
    )(*ins)


def shaped(shape, dtype=f32):
    return jax.ShapeDtypeStruct(shape, dtype)


def sketch_kernel(ids, part, *refs):
    grads, rights, keep, send, big, low = refs[:6], refs[6:10], refs[10], refs[11], refs[12], refs[13]
    z, core, shift = ids[1], ids[2], ids[3]
    for k in range(4):
        big[k], low[k] = split(rights[k][...])
    rows = keep.shape[0] // 4
    for out, half in ((keep, core), (send, 1 - core)):
        for b in range(4):
            at = pl.ds(pl.multiple_of(half * (4 * rows) + (z ^ b) * rows, 32), rows)
            total = part[at, :]
            for k, grad in zip((0, 1, 3, 2, 2, 3), grads):
                g = grad[at, :]
                total += mm(g, big[k ^ shift], ((1,), (0,)))
                total += mm(g, low[k ^ shift], ((1,), (0,)))
            out[b * rows : (b + 1) * rows, :] = total


def gram_kernel(ids, *refs):
    parts, other, grads = refs[:4], refs[4], refs[5:9]
    sketch, gram, t0, t1, t2, t3, big_t, low_t, flip, tokens = refs[9:]
    row, z, core, shift = ids[0], ids[1], ids[2], ids[3]
    rows = parts[0].shape[0]
    for k in range(4):
        at = pl.multiple_of((z ^ k) * rows, 32)
        sketch[pl.ds(core * (4 * rows) + at, rows), :] = parts[k][...]
        sketch[pl.ds((1 - core) * (4 * rows) + at, rows), :] = other[k * rows : (k + 1) * rows, :]
    s = sketch[...]
    gram[...] = mm(s, s, ((0,), (0,)), highest)
    big, low = split(s)
    for k in range(4):
        g = grads[k][...]
        tokens[k ^ shift] = mm(g, big, ((0,), (0,))) + mm(g, low, ((0,), (0,)))
    for j, ref in enumerate((t0, t1, t2, t3)):
        ref[...] = tokens[j]
    flip[...] = s.T
    size = flip.shape[0] // 8
    for i in range(8):
        at = pl.multiple_of(rank_block(row, i) * size, 32)
        b, l = split(flip[pl.ds(at, size), :])
        big_t[i * size : (i + 1) * size, :] = b
        low_t[i * size : (i + 1) * size, :] = l


def rank_block(row, i):
    upper, lower = (i // 2) % 2, i % 2
    if i < 4:
        return 2 * (upper ^ (row % 2)) + lower
    return 4 + 2 * (upper ^ (row // 2)) + lower


def side_kernel(big_t, low_t, momentum, top_keep, top_send, low_keep, low_send):
    mb, ml = split(momentum[...])
    total = mm(big_t[...], mb, ((1,), (0,)))
    total += mm(big_t[...], ml, ((1,), (0,)))
    total += mm(low_t[...], mb, ((1,), (0,)))
    n = top_keep.shape[0]
    for i, ref in enumerate((top_keep, top_send, low_keep, low_send)):
        ref[...] = total[i * n : (i + 1) * n, :]


def token_kernel(ids, own, other, inputs, *refs):
    before, after_refs, flip, tok = refs[:4], refs[4:8], refs[8], refs[9]
    row, core = ids[0], ids[2]
    half = own.shape[0]
    size = flip.shape[0] // 8

    @pl.when(pl.program_id(0) == 0)
    def _():
        for ref, place in ((own, core), (other, 1 - core)):
            flip[...] = ref[...].T
            for i in range(8):
                at = pl.multiple_of(rank_block(row, i) * size, 32)
                b, l = split(flip[pl.ds(at, size), :])
                tok[place, 0, i * size : (i + 1) * size, :] = b
                tok[place, 1, i * size : (i + 1) * size, :] = l

    total = 0.0
    for h in range(2):
        x = inputs[h * half : (h + 1) * half, :]
        total += mm(tok[h, 0], x, ((1,), (0,)))
        total += mm(tok[h, 1], x, ((1,), (0,)))
    for i, (old, new) in enumerate(zip(before, after_refs)):
        new[...] = old[...] + total[2 * i * size : 2 * (i + 1) * size, :]


def gradient_kernel(numbers, cuts, ids, *refs):
    count = len(numbers) // 2
    own, other, pieces = refs[:count], refs[count : 2 * count], list(refs[2 * count : -2])
    base, out = refs[-2], refs[-1]
    total = base[...]
    for at, number in enumerate(numbers):
        x = jnp.concatenate([pieces.pop(0)[...] for _ in range(number)], axis=0)
        cut = cuts[at // 2]
        grad = jnp.where(ids[2] == at % 2, own[at // 2][0, :, cut], other[at // 2][0, :, cut])
        total += mm(grad, x, ((1,), (0,)))
    out[...] = total


def right_kernel(n, ids, inverse, sketch, *refs):
    pieces, right, squares, basis, work = refs[:4], refs[4], refs[5], refs[6], refs[7]
    row = ids[0]
    size = work.shape[0] // 8

    @pl.when(pl.program_id(0) == 0)
    def _():
        sb, sl = split(sketch[...])
        ib, il = split(inverse[...])
        basis[...] = mm(sb, ib, ((1,), (1,))) + mm(sb, il, ((1,), (1,))) + mm(sl, ib, ((1,), (1,)))
        squares[...] = jnp.zeros_like(squares)

    place = 0
    for ref in pieces:
        for i in range(ref.shape[0] // size):
            at = pl.multiple_of(rank_block(row, place) * size, 32)
            work[pl.ds(at, size), :] = ref[i * size : (i + 1) * size, :]
            place += 1
    ib, il = split(inverse[...])
    tb, tl = split(work[...])
    total = mm(ib, tb, ((1,), (0,))) + mm(ib, tl, ((1,), (0,))) + mm(il, tb, ((1,), (0,)))
    right[...] = total
    at = pl.program_id(0) * total.shape[1] + lax.broadcasted_iota(jnp.int32, total.shape, 1)
    sb, sl = split(jnp.where(at < n, total * total, 0.0))
    ones = jnp.ones((8, total.shape[1]), bf16)
    squares[...] += mm(ones, sb, ((1,), (1,))) + mm(ones, sl, ((1,), (1,)))


def weights_kernel(n_total, factor, squares, basis, right, weights, out, factor_out, big, low):
    scale = lax.rsqrt(squares[0:1, :] / n_total + tiny_eps)

    @pl.when(pl.program_id(0) == 0)
    def _():
        big[...], low[...] = split(basis[...] * (scale * -factor))

    rb, rl = split(right[...])
    update = mm(big[...], rb, ((1,), (0,))) + mm(big[...], rl, ((1,), (0,))) + mm(low[...], rb, ((1,), (0,)))
    out[...] = weights[...].astype(f32) * (1.0 - step_rate * weight_decay) + update
    factor_out[...] = right[...].T * scale


def momentum_kernel(cut, ids, own, other, first, second, basis, right, base, out, small):
    @pl.when(pl.program_id(0) == 0)
    def _():
        small[...] = (basis[...] * -(1.0 - mix_rate)).astype(bf16)

    mine, its = own[0, :, cut], other[0, :, cut]
    total = base[...] + mm(jnp.where(ids[2] == 0, mine, its), first[...], ((1,), (0,)))
    total += mm(jnp.where(ids[2] == 0, its, mine), second[...], ((1,), (0,)))
    out[...] = total + mm(small[...], right[...].astype(bf16), ((1,), (0,)))


def swap(x, axis, bit):
    size = lax.axis_size(axis)
    return lax.ppermute(x, axis, [(i, i ^ bit) for i in range(size)])


def plane(n_total, m_total, inputs, out_grads, weights, momentum, right_factor):
    return plane_body(n_total, m_total, inputs, out_grads, weights, momentum, right_factor)


def line(x, inner):
    steps = ((1, 2), (2, 1)) if inner else ((1, 0), (2, 3))
    return lax.ppermute(x, "col", [(2 * a + h, 2 * b + h) for a, b in steps for h in range(2)])


def swaps(x, axis, unit):
    return [swap(x, axis, unit * k) for k in (1, 2, 3)]


def plane_body(n_total, m_total, inputs, out_grads, weights, momentum, right_factor):
    rank = right_factor.shape[1]
    row = lax.axis_index("row")
    col = lax.axis_index("col")
    core, z = col % 2, col // 2
    ids = jnp.stack([row, z, core, row ^ z]).astype(jnp.int32)
    tokens, n = inputs.shape
    m = momentum.shape[0]
    block = out_grads.shape[0]
    tn = tile_of(n)
    tiles = (pl.cdiv(n, tn),)

    def columns(rows):
        return pl.BlockSpec((rows, tn), lambda i, *_: (0, i))

    def fixed(*shape):
        return pl.BlockSpec(shape, lambda i, *_: (0,) * len(shape))

    def pick(j):
        return pl.BlockSpec((1, m, block), lambda i, ids: (ids[3] ^ j, 0, 0))

    grads = out_grads.T
    near = swap(grads, "col", 2)
    inner1 = line(grads, True)
    inner2 = line(near, True)
    outer1 = line(inner1, False)
    outer2 = line(inner2, False)
    own = [grads, near, inner2 + outer1, inner1 + outer2]

    in_right = mm(inputs.astype(f32), right_factor, ((1,), (0,)), high)
    keep = lax.dynamic_slice_in_dim(in_right, core * block, block, 0)
    send = lax.dynamic_slice_in_dim(in_right, (1 - core) * block, block, 0)
    in_right = keep + swap(send, "col", 1)
    rights = [in_right] + swaps(in_right, "row", 1)
    quarter = tokens // 4
    cut0, cut2 = inputs[:quarter], inputs[2 * quarter : 3 * quarter]
    cut1, cut3 = inputs[quarter : 2 * quarter], inputs[3 * quarter :]
    half0, half1 = inputs[: 2 * quarter], inputs[2 * quarter :]
    x0, y2 = swap(cut0, "row", 1), swap(cut2, "row", 2)
    x1, y3 = swap(cut1, "row", 1), swap(cut3, "row", 2)
    x23, y01 = swap(half1, "row", 1), swap(half0, "row", 2)
    other = [swap(g, "col", 1) for g in own]
    own_all = jnp.stack(own)
    other_all = jnp.stack(other)

    part = mm(momentum, right_factor, ((1,), (0,)), high)
    keep, send = call(
        sketch_kernel, (shaped((m // 2, rank)),) * 2, (ids, part, grads, near, inner1, inner2, outer1, outer2, *rights),
        [whole_smem] + [whole_vmem] * 11, (whole_vmem,) * 2,
        scratch=[pltpu.VMEM((4, block, rank), bf16)] * 2, flops=4 * m * 4 * block * rank, moved=8_000_000)
    mine = keep + swap(send, "col", 1)
    size = m // 8
    total = mine[:size]
    for k in (1, 2, 3):
        total = total + swap(mine[k * size : (k + 1) * size], "col", 2 * k)
    parts = [total] + swaps(total, "col", 2)
    rest = swap(jnp.concatenate(parts, axis=0), "col", 1)

    first_by_y, first_by_x = swap(x0, "row", 2), swap(y2, "row", 1)
    second_by_y, second_by_x = swap(x1, "row", 2), swap(y3, "row", 1)

    sketch, gram, *toks, big_t, low_t = call(
        gram_kernel,
        (shaped((m, rank)), shaped((rank, rank)), *([shaped((block, rank))] * 4), shaped((rank, m), bf16), shaped((rank, m), bf16)),
        (ids, *parts, rest, *own), [whole_smem] + [whole_vmem] * 9, (whole_vmem,) * 8,
        scratch=[pltpu.VMEM((rank, m), f32), pltpu.VMEM((4, block, rank), f32)], flops=20 * m * rank * rank, moved=8_000_000)
    token = toks[0]
    for k in (1, 2, 3):
        token = token + swap(toks[k], "row", k)
    token_other = swap(token, "col", 1)
    gram = gram + swap(gram, "row", 1)
    gram = gram + swap(gram, "row", 2)

    n8 = rank // 8
    sides = call(
        side_kernel, (shaped((rank // 4, n)),) * 4, (big_t, low_t, momentum),
        [whole_vmem] * 2 + [columns(m)], (columns(rank // 4),) * 4, tiles,
        flops=6 * m * n * rank, moved=5 * m * n)
    top, top_send, low, low_send = call(
        token_kernel, (shaped((2 * n8, n)),) * 4, (ids, token, token_other, inputs, *sides),
        [whole_smem] + [whole_vmem] * 2 + [columns(tokens)] + [columns(2 * n8)] * 4, (columns(2 * n8),) * 4, tiles,
        scratch=[pltpu.VMEM((rank, block), f32), pltpu.VMEM((2, 2, rank, block), bf16)],
        flops=4 * tokens * n * rank, moved=10 * rank * n)
    top, low = top + swap(top_send, "row", 1), low + swap(low_send, "row", 2)
    top, low = top + swap(top, "row", 2), low + swap(low, "row", 1)
    top_other, low_other = swap(top, "row", 1), swap(low, "row", 2)

    inverse = inverse_factor(gram)

    every, early, late = slice(None), slice(0, quarter), slice(quarter, 2 * quarter)

    def gradient(picks, numbers, cuts, pieces, base):
        return call(
            functools.partial(gradient_kernel, numbers, cuts), shaped((m, n)),
            (ids, *([own_all] * len(picks)), *([other_all] * len(picks)), *pieces, base),
            [pick(j) for j in picks] * 2 + [columns(x.shape[0]) for x in pieces] + [columns(m)], columns(m), tiles,
            flops=2 * m * n * sum(x.shape[0] for x in pieces), moved=8 * m * n, prefetch=1)

    moment = gradient((0, 1), (1, 1, 2, 1), (every, every), (half0, half1, x0, x1, x23), momentum)
    moment = gradient(
        (2, 3), (1, 2, 1, 1), (every, early), (y01, y2, y3, first_by_y, first_by_x), moment)

    right, squares, basis = call(
        functools.partial(right_kernel, n), (shaped((rank, n)), shaped((8, rank)), shaped((m, rank))),
        (ids, inverse, sketch, top, top_other, low, low_other),
        [whole_smem] + [whole_vmem] * 2 + [columns(2 * n8)] * 4,
        (columns(rank), fixed(8, rank), fixed(m, rank)), tiles,
        scratch=[pltpu.VMEM((rank, tn), f32)], flops=6 * n * rank * rank, moved=12 * n * rank)
    squares = squares + swap(squares, "col", 1)
    w1, w2, w3 = swaps(squares, "col", 2)
    squares = (squares + w1) + (w2 + w3)
    weights_new, factor_new = call(
        functools.partial(weights_kernel, n_total, step_rate * math.sqrt(m_total / rank)),
        (shaped((m, n)), shaped((n, rank))), (squares, basis, right, weights),
        [whole_vmem] * 2 + [columns(rank), columns(m)],
        (columns(m), pl.BlockSpec((tn, rank), lambda i, *_: (i, 0))), tiles,
        scratch=[pltpu.VMEM((m, rank), bf16)] * 2, flops=6 * m * n * rank, moved=6 * m * n)
    momentum_new = call(
        functools.partial(momentum_kernel, late), shaped((m, n)),
        (ids, own_all, other_all, second_by_y, second_by_x, basis, right, moment),
        [pick(3), pick(3), columns(quarter), columns(quarter), fixed(m, rank), columns(rank), columns(m)],
        columns(m), tiles, scratch=[pltpu.VMEM((m, rank), bf16)],
        flops=2 * m * n * (tokens // 2 + rank), moved=8 * m * n, prefetch=1, aliases={7: 0})
    return (weights_new, momentum_new, factor_new)


def solution(mesh):
    n_row, n_col = mesh.shape["row"], mesh.shape["col"]
    fast = (n_row, n_col) == (4, 8)
    body = plane if fast else general

    def whole(inputs, out_grads, weights, momentum, right_factor):
        m_total, n_total = weights.shape
        return jax.shard_map(
            functools.partial(body, n_total, m_total),
            mesh=mesh,
            in_specs=(P("row", "col"), P("col", "row"), P("row", "col"), P("row", "col"), P("col", None)),
            out_specs=(P("row", "col"), P("row", "col"), P("col", None)),
            check_vma=False,
        )(inputs, out_grads, weights, momentum, right_factor)

    return whole
```

```python
import functools
import math

import jax
import jax.numpy as jnp
from jax import lax
from jax.experimental import pallas as pl
from jax.experimental.pallas import tpu as pltpu
from jax.sharding import PartitionSpec as P


mix_rate = 0.95
step_rate = 0.3
weight_decay = 0.1
tiny_eps = 1e-06
highest = lax.Precision.HIGHEST
high = lax.Precision.HIGH
f32 = jnp.float32


def mm(a, b, dims, precision=None):
    return lax.dot_general(a, b, (dims, ((), ())), precision=precision, preferred_element_type=f32)


def general(n_total, m_total, inputs, out_grads, weights, momentum, right_factor):
    rank = right_factor.shape[1]
    grads_all = lax.all_gather(out_grads, "col", axis=0, tiled=True)
    inputs_all = lax.all_gather(inputs, "row", axis=0, tiled=True)
    moment = momentum + mm(grads_all, inputs_all, ((0,), (0,)))
    sketch = lax.psum(mm(moment, right_factor, ((1,), (0,)), highest), "col")
    gram = lax.psum(mm(sketch, sketch, ((0,), (0,)), highest), "row")
    inverse = inverse_factor(gram)
    basis = mm(sketch, inverse, ((1,), (1,)), highest)
    right_side = lax.psum(mm(moment, basis, ((0,), (0,)), highest), "row")
    squares = lax.psum(jnp.sum(right_side * right_side, axis=0), "col")
    factor_new = right_side * lax.rsqrt(squares / n_total + tiny_eps)
    momentum_new = moment - (1.0 - mix_rate) * mm(basis, right_side, ((1,), (1,)), highest)
    update = mm(basis, factor_new, ((1,), (1,)), highest)
    weights_new = (
        weights.astype(f32) * (1.0 - step_rate * weight_decay)
        - step_rate * math.sqrt(m_total / rank) * update
    )
    return (weights_new, momentum_new, factor_new)


def base_inverse(a):
    n = a.shape[0]
    rows = lax.broadcasted_iota(jnp.int32, (n, n), 0)
    cols = lax.broadcasted_iota(jnp.int32, (n, n), 1)
    left = a
    right = jnp.where(rows == cols, 1.0, 0.0).astype(f32)
    pivots = jnp.ones((n, n), f32)
    step = 8
    for start in range(0, n, step):
        columns = [jnp.broadcast_to(left[:, start + i : start + i + 1], (n, n)) for i in range(step)]
        for i in range(step):
            j = start + i
            pivot = jnp.broadcast_to(columns[i][j : j + 1, :], (n, n))
            pivots = jnp.where(rows == j, pivot, pivots)
            if j + 1 == n:
                break
            ratio = jnp.where(rows > j, columns[i] * (1.0 / pivot), 0.0)
            for k in range(i + 1, step):
                columns[k] = columns[k] - ratio * jnp.broadcast_to(columns[k][j : j + 1, :], (n, n))
            left = left - ratio * jnp.broadcast_to(left[j : j + 1, :], (n, n))
            right = right - ratio * jnp.broadcast_to(right[j : j + 1, :], (n, n))
    root = lax.rsqrt(pivots)
    return right * (root * (1.5 - 0.5 * pivots * root * root))


def inverse_kernel(gram_ref, out_ref, work_ref):
    n = gram_ref.shape[0]
    work_ref[...] = gram_ref[...]
    out_ref[...] = jnp.zeros_like(out_ref)

    def solve(at, size):
        span = slice(at, at + size)
        if size <= 32:
            out_ref[span, span] = base_inverse(work_ref[span, span])
            return
        half = size // 2
        one, two = slice(at, at + half), slice(at + half, at + size)
        solve(at, half)
        inv_one = out_ref[one, one]
        low = mm(work_ref[two, one], inv_one, ((1,), (1,)), highest)
        work_ref[two, two] = work_ref[two, two] - mm(low, low, ((1,), (1,)), highest)
        side = mm(low, inv_one, ((1,), (0,)), highest)
        solve(at + half, half)
        out_ref[two, one] = -mm(out_ref[two, two], side, ((1,), (0,)), highest)

    solve(0, n)


def inverse_factor(gram):
    return pl.pallas_call(
        inverse_kernel,
        out_shape=jax.ShapeDtypeStruct(gram.shape, f32),
        in_specs=[pl.BlockSpec(memory_space=pltpu.VMEM)],
        out_specs=pl.BlockSpec(memory_space=pltpu.VMEM),
        scratch_shapes=[pltpu.VMEM(gram.shape, f32)],
        cost_estimate=pl.CostEstimate(flops=20_000_000_000, bytes_accessed=10_000_000, transcendentals=0),
    )(gram)


bf16 = jnp.bfloat16
VMEM_MIB = 30
whole_vmem = pl.BlockSpec(memory_space=pltpu.VMEM)
whole_smem = pl.BlockSpec(memory_space=pltpu.SMEM)


def split(x):
    big = x.astype(bf16)
    return big, (x - big.astype(f32)).astype(bf16)


def tile_of(n):
    return min(n, 512)


def call(kernel, outs, ins, specs, out_specs, grid=(), scratch=(), flops=0, moved=0, aliases={}, prefetch=0, grant=VMEM_MIB):
    return pl.pallas_call(
        kernel,
        out_shape=outs,
        grid_spec=pltpu.PrefetchScalarGridSpec(
            num_scalar_prefetch=prefetch, grid=grid, in_specs=specs, out_specs=out_specs, scratch_shapes=list(scratch)
        ),
        input_output_aliases=aliases,
        compiler_params=pltpu.CompilerParams(vmem_limit_bytes=grant * 2**20),
        cost_estimate=pl.CostEstimate(flops=flops, bytes_accessed=moved, transcendentals=0),
    )(*ins)


def shaped(shape, dtype=f32):
    return jax.ShapeDtypeStruct(shape, dtype)


def sketch_kernel(ids, part, *refs):
    grads, rights, keep, send, big, low = refs[:6], refs[6:10], refs[10], refs[11], refs[12], refs[13]
    z, core, shift = ids[1], ids[2], ids[3]
    for k in range(4):
        big[k], low[k] = split(rights[k][...])
    rows = keep.shape[0] // 4
    for out, half in ((keep, core), (send, 1 - core)):
        for b in range(4):
            at = pl.ds(pl.multiple_of(half * (4 * rows) + (z ^ b) * rows, 32), rows)
            total = part[at, :]
            for k, grad in zip((0, 1, 3, 2, 2, 3), grads):
                g = grad[at, :]
                total += mm(g, big[k ^ shift], ((1,), (0,)))
                total += mm(g, low[k ^ shift], ((1,), (0,)))
            out[b * rows : (b + 1) * rows, :] = total


def gram_kernel(ids, *refs):
    parts, other, grads = refs[:4], refs[4], refs[5:9]
    sketch, gram, t0, t1, t2, t3, big_t, low_t, flip, tokens = refs[9:]
    row, z, core, shift = ids[0], ids[1], ids[2], ids[3]
    rows = parts[0].shape[0]
    for k in range(4):
        at = pl.multiple_of((z ^ k) * rows, 32)
        sketch[pl.ds(core * (4 * rows) + at, rows), :] = parts[k][...]
        sketch[pl.ds((1 - core) * (4 * rows) + at, rows), :] = other[k * rows : (k + 1) * rows, :]
    s = sketch[...]
    gram[...] = mm(s, s, ((0,), (0,)), highest)
    big, low = split(s)
    for k in range(4):
        g = grads[k][...]
        tokens[k ^ shift] = mm(g, big, ((0,), (0,))) + mm(g, low, ((0,), (0,)))
    for j, ref in enumerate((t0, t1, t2, t3)):
        ref[...] = tokens[j]
    flip[...] = s.T
    size = flip.shape[0] // 8
    for i in range(8):
        at = pl.multiple_of(rank_block(row, i) * size, 32)
        b, l = split(flip[pl.ds(at, size), :])
        big_t[i * size : (i + 1) * size, :] = b
        low_t[i * size : (i + 1) * size, :] = l


def rank_block(row, i):
    upper, lower = (i // 2) % 2, i % 2
    if i < 4:
        return 2 * (upper ^ (row % 2)) + lower
    return 4 + 2 * (upper ^ (row // 2)) + lower


def side_kernel(big_t, low_t, momentum, top_keep, top_send, low_keep, low_send):
    mb, ml = split(momentum[...])
    total = mm(big_t[...], mb, ((1,), (0,)))
    total += mm(big_t[...], ml, ((1,), (0,)))
    total += mm(low_t[...], mb, ((1,), (0,)))
    n = top_keep.shape[0]
    for i, ref in enumerate((top_keep, top_send, low_keep, low_send)):
        ref[...] = total[i * n : (i + 1) * n, :]


def token_kernel(ids, own, other, inputs, *refs):
    before, after_refs, flip, tok = refs[:4], refs[4:8], refs[8], refs[9]
    row, core = ids[0], ids[2]
    half = own.shape[0]
    size = flip.shape[0] // 8

    @pl.when(pl.program_id(0) == 0)
    def _():
        for ref, place in ((own, core), (other, 1 - core)):
            flip[...] = ref[...].T
            for i in range(8):
                at = pl.multiple_of(rank_block(row, i) * size, 32)
                b, l = split(flip[pl.ds(at, size), :])
                tok[place, 0, i * size : (i + 1) * size, :] = b
                tok[place, 1, i * size : (i + 1) * size, :] = l

    total = 0.0
    for h in range(2):
        x = inputs[h * half : (h + 1) * half, :]
        total += mm(tok[h, 0], x, ((1,), (0,)))
        total += mm(tok[h, 1], x, ((1,), (0,)))
    for i, (old, new) in enumerate(zip(before, after_refs)):
        new[...] = old[...] + total[2 * i * size : 2 * (i + 1) * size, :]


def gradient_kernel(numbers, cuts, ids, *refs):
    count = len(numbers) // 2
    own, other, pieces = refs[:count], refs[count : 2 * count], list(refs[2 * count : -2])
    base, out = refs[-2], refs[-1]
    total = base[...]
    for at, number in enumerate(numbers):
        x = jnp.concatenate([pieces.pop(0)[...] for _ in range(number)], axis=0)
        cut = cuts[at // 2]
        grad = jnp.where(ids[2] == at % 2, own[at // 2][0, :, cut], other[at // 2][0, :, cut])
        total += mm(grad, x, ((1,), (0,)))
    out[...] = total


def right_kernel(n, ids, inverse, sketch, *refs):
    pieces, right, squares, basis, work = refs[:4], refs[4], refs[5], refs[6], refs[7]
    row = ids[0]
    size = work.shape[0] // 8

    @pl.when(pl.program_id(0) == 0)
    def _():
        sb, sl = split(sketch[...])
        ib, il = split(inverse[...])
        basis[...] = mm(sb, ib, ((1,), (1,))) + mm(sb, il, ((1,), (1,))) + mm(sl, ib, ((1,), (1,)))
        squares[...] = jnp.zeros_like(squares)

    place = 0
    for ref in pieces:
        for i in range(ref.shape[0] // size):
            at = pl.multiple_of(rank_block(row, place) * size, 32)
            work[pl.ds(at, size), :] = ref[i * size : (i + 1) * size, :]
            place += 1
    ib, il = split(inverse[...])
    tb, tl = split(work[...])
    total = mm(ib, tb, ((1,), (0,))) + mm(ib, tl, ((1,), (0,))) + mm(il, tb, ((1,), (0,)))
    right[...] = total
    at = pl.program_id(0) * total.shape[1] + lax.broadcasted_iota(jnp.int32, total.shape, 1)
    sb, sl = split(jnp.where(at < n, total * total, 0.0))
    ones = jnp.ones((8, total.shape[1]), bf16)
    squares[...] += mm(ones, sb, ((1,), (1,))) + mm(ones, sl, ((1,), (1,)))


def weights_kernel(n_total, factor, squares, basis, right, weights, out, factor_out, big, low):
    scale = lax.rsqrt(squares[0:1, :] / n_total + tiny_eps)

    @pl.when(pl.program_id(0) == 0)
    def _():
        big[...], low[...] = split(basis[...] * (scale * -factor))

    rb, rl = split(right[...])
    update = mm(big[...], rb, ((1,), (0,))) + mm(big[...], rl, ((1,), (0,))) + mm(low[...], rb, ((1,), (0,)))
    out[...] = weights[...].astype(f32) * (1.0 - step_rate * weight_decay) + update
    factor_out[...] = right[...].T * scale


def momentum_kernel(cut, ids, own, other, first, second, basis, right, base, out, small):
    @pl.when(pl.program_id(0) == 0)
    def _():
        small[...] = (basis[...] * -(1.0 - mix_rate)).astype(bf16)

    mine, its = own[0, :, cut], other[0, :, cut]
    total = base[...] + mm(jnp.where(ids[2] == 0, mine, its), first[...], ((1,), (0,)))
    total += mm(jnp.where(ids[2] == 0, its, mine), second[...], ((1,), (0,)))
    out[...] = total + mm(small[...], right[...].astype(bf16), ((1,), (0,)))


def swap(x, axis, bit):
    size = lax.axis_size(axis)
    return lax.ppermute(x, axis, [(i, i ^ bit) for i in range(size)])


def plane(n_total, m_total, inputs, out_grads, weights, momentum, right_factor):
    return plane_body(n_total, m_total, inputs, out_grads, weights, momentum, right_factor)


def line(x, inner):
    steps = ((1, 2), (2, 1)) if inner else ((1, 0), (2, 3))
    return lax.ppermute(x, "col", [(2 * a + h, 2 * b + h) for a, b in steps for h in range(2)])


def swaps(x, axis, unit):
    return [swap(x, axis, unit * k) for k in (1, 2, 3)]


def plane_body(n_total, m_total, inputs, out_grads, weights, momentum, right_factor):
    rank = right_factor.shape[1]
    row = lax.axis_index("row")
    col = lax.axis_index("col")
    core, z = col % 2, col // 2
    ids = jnp.stack([row, z, core, row ^ z]).astype(jnp.int32)
    tokens, n = inputs.shape
    m = momentum.shape[0]
    block = out_grads.shape[0]
    tn = tile_of(n)
    tiles = (pl.cdiv(n, tn),)

    def columns(rows):
        return pl.BlockSpec((rows, tn), lambda i, *_: (0, i))

    def fixed(*shape):
        return pl.BlockSpec(shape, lambda i, *_: (0,) * len(shape))

    def pick(j):
        return pl.BlockSpec((1, m, block), lambda i, ids: (ids[3] ^ j, 0, 0))

    grads = out_grads.T
    near = swap(grads, "col", 2)
    inner1 = line(grads, True)
    inner2 = line(near, True)
    outer1 = line(inner1, False)
    outer2 = line(inner2, False)
    own = [grads, near, inner2 + outer1, inner1 + outer2]

    in_right = mm(inputs.astype(f32), right_factor, ((1,), (0,)), high)
    keep = lax.dynamic_slice_in_dim(in_right, core * block, block, 0)
    send = lax.dynamic_slice_in_dim(in_right, (1 - core) * block, block, 0)
    in_right = keep + swap(send, "col", 1)
    rights = [in_right] + swaps(in_right, "row", 1)
    quarter = tokens // 4
    cut0, cut2 = inputs[:quarter], inputs[2 * quarter : 3 * quarter]
    cut1, cut3 = inputs[quarter : 2 * quarter], inputs[3 * quarter :]
    half0, half1 = inputs[: 2 * quarter], inputs[2 * quarter :]
    x0, y2 = swap(cut0, "row", 1), swap(cut2, "row", 2)
    x1, y3 = swap(cut1, "row", 1), swap(cut3, "row", 2)
    x23, y01 = swap(half1, "row", 1), swap(half0, "row", 2)
    other = [swap(g, "col", 1) for g in own]
    own_all = jnp.stack(own)
    other_all = jnp.stack(other)

    part = mm(momentum, right_factor, ((1,), (0,)), high)
    keep, send = call(
        sketch_kernel, (shaped((m // 2, rank)),) * 2, (ids, part, grads, near, inner1, inner2, outer1, outer2, *rights),
        [whole_smem] + [whole_vmem] * 11, (whole_vmem,) * 2,
        scratch=[pltpu.VMEM((4, block, rank), bf16)] * 2, flops=4 * m * 4 * block * rank, moved=8_000_000)
    mine = keep + swap(send, "col", 1)
    size = m // 8
    total = mine[:size]
    for k in (1, 2, 3):
        total = total + swap(mine[k * size : (k + 1) * size], "col", 2 * k)
    parts = [total] + swaps(total, "col", 2)
    rest = swap(jnp.concatenate(parts, axis=0), "col", 1)

    first_by_y, first_by_x = swap(x0, "row", 2), swap(y2, "row", 1)
    second_by_y, second_by_x = swap(x1, "row", 2), swap(y3, "row", 1)

    sketch, gram, *toks, big_t, low_t = call(
        gram_kernel,
        (shaped((m, rank)), shaped((rank, rank)), *([shaped((block, rank))] * 4), shaped((rank, m), bf16), shaped((rank, m), bf16)),
        (ids, *parts, rest, *own), [whole_smem] + [whole_vmem] * 9, (whole_vmem,) * 8,
        scratch=[pltpu.VMEM((rank, m), f32), pltpu.VMEM((4, block, rank), f32)], flops=20 * m * rank * rank, moved=8_000_000)
    token = toks[0]
    for k in (1, 2, 3):
        token = token + swap(toks[k], "row", k)
    token_other = swap(token, "col", 1)
    gram = gram + swap(gram, "row", 1)
    gram = gram + swap(gram, "row", 2)

    n8 = rank // 8
    sides = call(
        side_kernel, (shaped((rank // 4, n)),) * 4, (big_t, low_t, momentum),
        [whole_vmem] * 2 + [columns(m)], (columns(rank // 4),) * 4, tiles,
        flops=6 * m * n * rank, moved=5 * m * n, grant=40)
    top, top_send, low, low_send = call(
        token_kernel, (shaped((2 * n8, n)),) * 4, (ids, token, token_other, inputs, *sides),
        [whole_smem] + [whole_vmem] * 2 + [columns(tokens)] + [columns(2 * n8)] * 4, (columns(2 * n8),) * 4, tiles,
        scratch=[pltpu.VMEM((rank, block), f32), pltpu.VMEM((2, 2, rank, block), bf16)],
        flops=4 * tokens * n * rank, moved=10 * rank * n)
    top, low = top + swap(top_send, "row", 1), low + swap(low_send, "row", 2)
    top, low = top + swap(top, "row", 2), low + swap(low, "row", 1)
    top_other, low_other = swap(top, "row", 1), swap(low, "row", 2)

    inverse = inverse_factor(gram)

    every, early, late = slice(None), slice(0, quarter), slice(quarter, 2 * quarter)

    def gradient(picks, numbers, cuts, pieces, base):
        return call(
            functools.partial(gradient_kernel, numbers, cuts), shaped((m, n)),
            (ids, *([own_all] * len(picks)), *([other_all] * len(picks)), *pieces, base),
            [pick(j) for j in picks] * 2 + [columns(x.shape[0]) for x in pieces] + [columns(m)], columns(m), tiles,
            flops=2 * m * n * sum(x.shape[0] for x in pieces), moved=8 * m * n, prefetch=1)

    moment = gradient((0, 1), (1, 1, 2, 1), (every, every), (half0, half1, x0, x1, x23), momentum)
    moment = gradient(
        (2, 3), (1, 2, 1, 1), (every, early), (y01, y2, y3, first_by_y, first_by_x), moment)

    right, squares, basis = call(
        functools.partial(right_kernel, n), (shaped((rank, n)), shaped((8, rank)), shaped((m, rank))),
        (ids, inverse, sketch, top, top_other, low, low_other),
        [whole_smem] + [whole_vmem] * 2 + [columns(2 * n8)] * 4,
        (columns(rank), fixed(8, rank), fixed(m, rank)), tiles,
        scratch=[pltpu.VMEM((rank, tn), f32)], flops=6 * n * rank * rank, moved=12 * n * rank)
    squares = squares + swap(squares, "col", 1)
    w1, w2, w3 = swaps(squares, "col", 2)
    squares = (squares + w1) + (w2 + w3)
    weights_new, factor_new = call(
        functools.partial(weights_kernel, n_total, step_rate * math.sqrt(m_total / rank)),
        (shaped((m, n)), shaped((n, rank))), (squares, basis, right, weights),
        [whole_vmem] * 2 + [columns(rank), columns(m)],
        (columns(m), pl.BlockSpec((tn, rank), lambda i, *_: (i, 0))), tiles,
        scratch=[pltpu.VMEM((m, rank), bf16)] * 2, flops=6 * m * n * rank, moved=6 * m * n)
    momentum_new = call(
        functools.partial(momentum_kernel, late), shaped((m, n)),
        (ids, own_all, other_all, second_by_y, second_by_x, basis, right, moment),
        [pick(3), pick(3), columns(quarter), columns(quarter), fixed(m, rank), columns(rank), columns(m)],
        columns(m), tiles, scratch=[pltpu.VMEM((m, rank), bf16)],
        flops=2 * m * n * (tokens // 2 + rank), moved=8 * m * n, prefetch=1, aliases={7: 0})
    return (weights_new, momentum_new, factor_new)


def solution(mesh):
    n_row, n_col = mesh.shape["row"], mesh.shape["col"]
    fast = (n_row, n_col) == (4, 8)
    body = plane if fast else general

    def whole(inputs, out_grads, weights, momentum, right_factor):
        m_total, n_total = weights.shape
        return jax.shard_map(
            functools.partial(body, n_total, m_total),
            mesh=mesh,
            in_specs=(P("row", "col"), P("col", "row"), P("row", "col"), P("row", "col"), P("col", None)),
            out_specs=(P("row", "col"), P("row", "col"), P("col", None)),
            check_vma=False,
        )(inputs, out_grads, weights, momentum, right_factor)

    return whole
```

```python
import functools
import math

import jax
import jax.numpy as jnp
from jax import lax
from jax.experimental import pallas as pl
from jax.experimental.pallas import tpu as pltpu
from jax.sharding import PartitionSpec as P


mix_rate = 0.95
step_rate = 0.3
weight_decay = 0.1
tiny_eps = 1e-06
highest = lax.Precision.HIGHEST
high = lax.Precision.HIGH
f32 = jnp.float32


def mm(a, b, dims, precision=None):
    return lax.dot_general(a, b, (dims, ((), ())), precision=precision, preferred_element_type=f32)


def general(n_total, m_total, inputs, out_grads, weights, momentum, right_factor):
    rank = right_factor.shape[1]
    grads_all = lax.all_gather(out_grads, "col", axis=0, tiled=True)
    inputs_all = lax.all_gather(inputs, "row", axis=0, tiled=True)
    moment = momentum + mm(grads_all, inputs_all, ((0,), (0,)))
    sketch = lax.psum(mm(moment, right_factor, ((1,), (0,)), highest), "col")
    gram = lax.psum(mm(sketch, sketch, ((0,), (0,)), highest), "row")
    inverse = inverse_factor(gram)
    basis = mm(sketch, inverse, ((1,), (1,)), highest)
    right_side = lax.psum(mm(moment, basis, ((0,), (0,)), highest), "row")
    squares = lax.psum(jnp.sum(right_side * right_side, axis=0), "col")
    factor_new = right_side * lax.rsqrt(squares / n_total + tiny_eps)
    momentum_new = moment - (1.0 - mix_rate) * mm(basis, right_side, ((1,), (1,)), highest)
    update = mm(basis, factor_new, ((1,), (1,)), highest)
    weights_new = (
        weights.astype(f32) * (1.0 - step_rate * weight_decay)
        - step_rate * math.sqrt(m_total / rank) * update
    )
    return (weights_new, momentum_new, factor_new)


def base_inverse(a):
    n = a.shape[0]
    rows = lax.broadcasted_iota(jnp.int32, (n, n), 0)
    cols = lax.broadcasted_iota(jnp.int32, (n, n), 1)
    left = a
    right = jnp.where(rows == cols, 1.0, 0.0).astype(f32)
    pivots = jnp.ones((n, n), f32)
    step = 8
    for start in range(0, n, step):
        columns = [jnp.broadcast_to(left[:, start + i : start + i + 1], (n, n)) for i in range(step)]
        for i in range(step):
            j = start + i
            pivot = jnp.broadcast_to(columns[i][j : j + 1, :], (n, n))
            pivots = jnp.where(rows == j, pivot, pivots)
            if j + 1 == n:
                break
            ratio = jnp.where(rows > j, columns[i] * (1.0 / pivot), 0.0)
            for k in range(i + 1, step):
                columns[k] = columns[k] - ratio * jnp.broadcast_to(columns[k][j : j + 1, :], (n, n))
            left = left - ratio * jnp.broadcast_to(left[j : j + 1, :], (n, n))
            right = right - ratio * jnp.broadcast_to(right[j : j + 1, :], (n, n))
    root = lax.rsqrt(pivots)
    return right * (root * (1.5 - 0.5 * pivots * root * root))


def inverse_kernel(gram_ref, out_ref, work_ref):
    n = gram_ref.shape[0]
    work_ref[...] = gram_ref[...]
    out_ref[...] = jnp.zeros_like(out_ref)

    def solve(at, size):
        span = slice(at, at + size)
        if size <= 32:
            out_ref[span, span] = base_inverse(work_ref[span, span])
            return
        half = size // 2
        one, two = slice(at, at + half), slice(at + half, at + size)
        solve(at, half)
        inv_one = out_ref[one, one]
        low = mm(work_ref[two, one], inv_one, ((1,), (1,)), highest)
        work_ref[two, two] = work_ref[two, two] - mm(low, low, ((1,), (1,)), highest)
        side = mm(low, inv_one, ((1,), (0,)), highest)
        solve(at + half, half)
        out_ref[two, one] = -mm(out_ref[two, two], side, ((1,), (0,)), highest)

    solve(0, n)


def inverse_factor(gram):
    return pl.pallas_call(
        inverse_kernel,
        out_shape=jax.ShapeDtypeStruct(gram.shape, f32),
        in_specs=[pl.BlockSpec(memory_space=pltpu.VMEM)],
        out_specs=pl.BlockSpec(memory_space=pltpu.VMEM),
        scratch_shapes=[pltpu.VMEM(gram.shape, f32)],
        cost_estimate=pl.CostEstimate(flops=20_000_000_000, bytes_accessed=10_000_000, transcendentals=0),
    )(gram)


bf16 = jnp.bfloat16
VMEM_MIB = 30
whole_vmem = pl.BlockSpec(memory_space=pltpu.VMEM)
whole_smem = pl.BlockSpec(memory_space=pltpu.SMEM)


def split(x):
    big = x.astype(bf16)
    return big, (x - big.astype(f32)).astype(bf16)


def tile_of(n):
    return min(n, 512)


def call(kernel, outs, ins, specs, out_specs, grid=(), scratch=(), flops=0, moved=0, aliases={}, prefetch=0, grant=VMEM_MIB):
    return pl.pallas_call(
        kernel,
        out_shape=outs,
        grid_spec=pltpu.PrefetchScalarGridSpec(
            num_scalar_prefetch=prefetch, grid=grid, in_specs=specs, out_specs=out_specs, scratch_shapes=list(scratch)
        ),
        input_output_aliases=aliases,
        compiler_params=pltpu.CompilerParams(vmem_limit_bytes=grant * 2**20),
        cost_estimate=pl.CostEstimate(flops=flops, bytes_accessed=moved, transcendentals=0),
    )(*ins)


def shaped(shape, dtype=f32):
    return jax.ShapeDtypeStruct(shape, dtype)


def sketch_kernel(ids, part, *refs):
    grads, rights, keep, send, big, low = refs[:6], refs[6:10], refs[10], refs[11], refs[12], refs[13]
    z, core, shift = ids[1], ids[2], ids[3]
    for k in range(4):
        big[k], low[k] = split(rights[k][...])
    rows = keep.shape[0] // 4
    for out, half in ((keep, core), (send, 1 - core)):
        for b in range(4):
            at = pl.ds(pl.multiple_of(half * (4 * rows) + (z ^ b) * rows, 32), rows)
            total = part[at, :]
            for k, grad in zip((0, 1, 3, 2, 2, 3), grads):
                g = grad[at, :]
                total += mm(g, big[k ^ shift], ((1,), (0,)))
                total += mm(g, low[k ^ shift], ((1,), (0,)))
            out[b * rows : (b + 1) * rows, :] = total


def gram_kernel(ids, *refs):
    parts, other, grads = refs[:4], refs[4], refs[5:9]
    sketch, gram, t0, t1, t2, t3, big_t, low_t, flip, tokens = refs[9:]
    row, z, core, shift = ids[0], ids[1], ids[2], ids[3]
    rows = parts[0].shape[0]
    for k in range(4):
        at = pl.multiple_of((z ^ k) * rows, 32)
        sketch[pl.ds(core * (4 * rows) + at, rows), :] = parts[k][...]
        sketch[pl.ds((1 - core) * (4 * rows) + at, rows), :] = other[k * rows : (k + 1) * rows, :]
    s = sketch[...]
    gram[...] = mm(s, s, ((0,), (0,)), highest)
    big, low = split(s)
    for k in range(4):
        g = grads[k][...]
        tokens[k ^ shift] = mm(g, big, ((0,), (0,))) + mm(g, low, ((0,), (0,)))
    for j, ref in enumerate((t0, t1, t2, t3)):
        ref[...] = tokens[j]
    flip[...] = s.T
    size = flip.shape[0] // 8
    for i in range(8):
        at = pl.multiple_of(rank_block(row, i) * size, 32)
        b, l = split(flip[pl.ds(at, size), :])
        big_t[i * size : (i + 1) * size, :] = b
        low_t[i * size : (i + 1) * size, :] = l


def rank_block(row, i):
    upper, lower = (i // 2) % 2, i % 2
    if i < 4:
        return 2 * (upper ^ (row % 2)) + lower
    return 4 + 2 * (upper ^ (row // 2)) + lower


def side_kernel(big_t, low_t, momentum, top_keep, top_send, low_keep, low_send):
    mb, ml = split(momentum[...])
    total = mm(big_t[...], mb, ((1,), (0,)))
    total += mm(big_t[...], ml, ((1,), (0,)))
    total += mm(low_t[...], mb, ((1,), (0,)))
    n = top_keep.shape[0]
    for i, ref in enumerate((top_keep, top_send, low_keep, low_send)):
        ref[...] = total[i * n : (i + 1) * n, :]


def token_kernel(ids, own, other, inputs, *refs):
    before, after_refs, flip, tok = refs[:4], refs[4:8], refs[8], refs[9]
    row, core = ids[0], ids[2]
    half = own.shape[0]
    size = flip.shape[0] // 8

    @pl.when(pl.program_id(0) == 0)
    def _():
        for ref, place in ((own, core), (other, 1 - core)):
            flip[...] = ref[...].T
            for i in range(8):
                at = pl.multiple_of(rank_block(row, i) * size, 32)
                b, l = split(flip[pl.ds(at, size), :])
                tok[place, 0, i * size : (i + 1) * size, :] = b
                tok[place, 1, i * size : (i + 1) * size, :] = l

    total = 0.0
    for h in range(2):
        x = inputs[h * half : (h + 1) * half, :]
        total += mm(tok[h, 0], x, ((1,), (0,)))
        total += mm(tok[h, 1], x, ((1,), (0,)))
    for i, (old, new) in enumerate(zip(before, after_refs)):
        new[...] = old[...] + total[2 * i * size : 2 * (i + 1) * size, :]


def gradient_kernel(numbers, cuts, ids, *refs):
    count = len(numbers) // 2
    own, other, pieces = refs[:count], refs[count : 2 * count], list(refs[2 * count : -2])
    base, out = refs[-2], refs[-1]
    total = base[...]
    for j, cut in enumerate(cuts):
        x = [jnp.concatenate([pieces.pop(0)[...] for _ in range(numbers[2 * j + h])], axis=0) for h in range(2)]
        mine, its = own[j][0, :, cut], other[j][0, :, cut]
        grads = [jnp.where(ids[2] == 0, mine, its), jnp.where(ids[2] == 0, its, mine)]
        if cut == slice(None):
            total += mm(grads[0], x[0], ((1,), (0,)))
            total += mm(grads[1], x[1], ((1,), (0,)))
        else:
            total += mm(jnp.concatenate(grads, axis=1), jnp.concatenate(x, axis=0), ((1,), (0,)))
    out[...] = total


def right_kernel(n, ids, inverse, sketch, *refs):
    pieces, right, squares, basis, work = refs[:4], refs[4], refs[5], refs[6], refs[7]
    row = ids[0]
    size = work.shape[0] // 8

    @pl.when(pl.program_id(0) == 0)
    def _():
        sb, sl = split(sketch[...])
        ib, il = split(inverse[...])
        basis[...] = mm(sb, ib, ((1,), (1,))) + mm(sb, il, ((1,), (1,))) + mm(sl, ib, ((1,), (1,)))
        squares[...] = jnp.zeros_like(squares)

    place = 0
    for ref in pieces:
        for i in range(ref.shape[0] // size):
            at = pl.multiple_of(rank_block(row, place) * size, 32)
            work[pl.ds(at, size), :] = ref[i * size : (i + 1) * size, :]
            place += 1
    ib, il = split(inverse[...])
    tb, tl = split(work[...])
    total = mm(ib, tb, ((1,), (0,))) + mm(ib, tl, ((1,), (0,))) + mm(il, tb, ((1,), (0,)))
    right[...] = total
    at = pl.program_id(0) * total.shape[1] + lax.broadcasted_iota(jnp.int32, total.shape, 1)
    sb, sl = split(jnp.where(at < n, total * total, 0.0))
    ones = jnp.ones((8, total.shape[1]), bf16)
    squares[...] += mm(ones, sb, ((1,), (1,))) + mm(ones, sl, ((1,), (1,)))


def weights_kernel(n_total, factor, squares, basis, right, weights, out, factor_out, big, low):
    scale = lax.rsqrt(squares[0:1, :] / n_total + tiny_eps)

    @pl.when(pl.program_id(0) == 0)
    def _():
        big[...], low[...] = split(basis[...] * (scale * -factor))

    rb, rl = split(right[...])
    update = mm(big[...], rb, ((1,), (0,))) + mm(big[...], rl, ((1,), (0,))) + mm(low[...], rb, ((1,), (0,)))
    out[...] = weights[...].astype(f32) * (1.0 - step_rate * weight_decay) + update
    factor_out[...] = right[...].T * scale


def momentum_kernel(cut, ids, own, other, first, second, basis, right, base, out, small):
    @pl.when(pl.program_id(0) == 0)
    def _():
        small[...] = (basis[...] * -(1.0 - mix_rate)).astype(bf16)

    mine, its = own[0, :, cut], other[0, :, cut]
    grads = jnp.concatenate([jnp.where(ids[2] == 0, mine, its), jnp.where(ids[2] == 0, its, mine)], axis=1)
    total = base[...] + mm(grads, jnp.concatenate([first[...], second[...]], axis=0), ((1,), (0,)))
    out[...] = total + mm(small[...], right[...].astype(bf16), ((1,), (0,)))


def swap(x, axis, bit):
    size = lax.axis_size(axis)
    return lax.ppermute(x, axis, [(i, i ^ bit) for i in range(size)])


def plane(n_total, m_total, inputs, out_grads, weights, momentum, right_factor):
    return plane_body(n_total, m_total, inputs, out_grads, weights, momentum, right_factor)


def line(x, inner):
    steps = ((1, 2), (2, 1)) if inner else ((1, 0), (2, 3))
    return lax.ppermute(x, "col", [(2 * a + h, 2 * b + h) for a, b in steps for h in range(2)])


def swaps(x, axis, unit):
    return [swap(x, axis, unit * k) for k in (1, 2, 3)]


def plane_body(n_total, m_total, inputs, out_grads, weights, momentum, right_factor):
    rank = right_factor.shape[1]
    row = lax.axis_index("row")
    col = lax.axis_index("col")
    core, z = col % 2, col // 2
    ids = jnp.stack([row, z, core, row ^ z]).astype(jnp.int32)
    tokens, n = inputs.shape
    m = momentum.shape[0]
    block = out_grads.shape[0]
    tn = tile_of(n)
    tiles = (pl.cdiv(n, tn),)

    def columns(rows):
        return pl.BlockSpec((rows, tn), lambda i, *_: (0, i))

    def fixed(*shape):
        return pl.BlockSpec(shape, lambda i, *_: (0,) * len(shape))

    def pick(j):
        return pl.BlockSpec((1, m, block), lambda i, ids: (ids[3] ^ j, 0, 0))

    grads = out_grads.T
    near = swap(grads, "col", 2)
    inner1 = line(grads, True)
    inner2 = line(near, True)
    outer1 = line(inner1, False)
    outer2 = line(inner2, False)
    own = [grads, near, inner2 + outer1, inner1 + outer2]

    in_right = mm(inputs.astype(f32), right_factor, ((1,), (0,)), high)
    keep = lax.dynamic_slice_in_dim(in_right, core * block, block, 0)
    send = lax.dynamic_slice_in_dim(in_right, (1 - core) * block, block, 0)
    in_right = keep + swap(send, "col", 1)
    rights = [in_right] + swaps(in_right, "row", 1)
    quarter = tokens // 4
    cut0, cut2 = inputs[:quarter], inputs[2 * quarter : 3 * quarter]
    cut1, cut3 = inputs[quarter : 2 * quarter], inputs[3 * quarter :]
    half0, half1 = inputs[: 2 * quarter], inputs[2 * quarter :]
    x0, y2 = swap(cut0, "row", 1), swap(cut2, "row", 2)
    x1, y3 = swap(cut1, "row", 1), swap(cut3, "row", 2)
    x23, y01 = swap(half1, "row", 1), swap(half0, "row", 2)
    other = [swap(g, "col", 1) for g in own]
    own_all = jnp.stack(own)
    other_all = jnp.stack(other)

    part = mm(momentum, right_factor, ((1,), (0,)), high)
    keep, send = call(
        sketch_kernel, (shaped((m // 2, rank)),) * 2, (ids, part, grads, near, inner1, inner2, outer1, outer2, *rights),
        [whole_smem] + [whole_vmem] * 11, (whole_vmem,) * 2,
        scratch=[pltpu.VMEM((4, block, rank), bf16)] * 2, flops=4 * m * 4 * block * rank, moved=8_000_000)
    mine = keep + swap(send, "col", 1)
    size = m // 8
    total = mine[:size]
    for k in (1, 2, 3):
        total = total + swap(mine[k * size : (k + 1) * size], "col", 2 * k)
    parts = [total] + swaps(total, "col", 2)
    rest = swap(jnp.concatenate(parts, axis=0), "col", 1)

    first_by_y, first_by_x = swap(x0, "row", 2), swap(y2, "row", 1)
    second_by_y, second_by_x = swap(x1, "row", 2), swap(y3, "row", 1)

    sketch, gram, *toks, big_t, low_t = call(
        gram_kernel,
        (shaped((m, rank)), shaped((rank, rank)), *([shaped((block, rank))] * 4), shaped((rank, m), bf16), shaped((rank, m), bf16)),
        (ids, *parts, rest, *own), [whole_smem] + [whole_vmem] * 9, (whole_vmem,) * 8,
        scratch=[pltpu.VMEM((rank, m), f32), pltpu.VMEM((4, block, rank), f32)], flops=20 * m * rank * rank, moved=8_000_000)
    token = toks[0]
    for k in (1, 2, 3):
        token = token + swap(toks[k], "row", k)
    token_other = swap(token, "col", 1)
    gram = gram + swap(gram, "row", 1)
    gram = gram + swap(gram, "row", 2)

    n8 = rank // 8
    sides = call(
        side_kernel, (shaped((rank // 4, n)),) * 4, (big_t, low_t, momentum),
        [whole_vmem] * 2 + [columns(m)], (columns(rank // 4),) * 4, tiles,
        flops=6 * m * n * rank, moved=5 * m * n, grant=40)
    top, top_send, low, low_send = call(
        token_kernel, (shaped((2 * n8, n)),) * 4, (ids, token, token_other, inputs, *sides),
        [whole_smem] + [whole_vmem] * 2 + [columns(tokens)] + [columns(2 * n8)] * 4, (columns(2 * n8),) * 4, tiles,
        scratch=[pltpu.VMEM((rank, block), f32), pltpu.VMEM((2, 2, rank, block), bf16)],
        flops=4 * tokens * n * rank, moved=10 * rank * n)
    top, low = top + swap(top_send, "row", 1), low + swap(low_send, "row", 2)
    top, low = top + swap(top, "row", 2), low + swap(low, "row", 1)
    top_other, low_other = swap(top, "row", 1), swap(low, "row", 2)

    inverse = inverse_factor(gram)

    every, early, late = slice(None), slice(0, quarter), slice(quarter, 2 * quarter)

    def gradient(picks, numbers, cuts, pieces, base):
        return call(
            functools.partial(gradient_kernel, numbers, cuts), shaped((m, n)),
            (ids, *([own_all] * len(picks)), *([other_all] * len(picks)), *pieces, base),
            [pick(j) for j in picks] * 2 + [columns(x.shape[0]) for x in pieces] + [columns(m)], columns(m), tiles,
            flops=2 * m * n * sum(x.shape[0] for x in pieces), moved=8 * m * n, prefetch=1)

    moment = gradient((0, 1), (1, 1, 2, 1), (every, every), (half0, half1, x0, x1, x23), momentum)
    moment = gradient(
        (2, 3), (1, 2, 1, 1), (every, early), (y01, y2, y3, first_by_y, first_by_x), moment)

    right, squares, basis = call(
        functools.partial(right_kernel, n), (shaped((rank, n)), shaped((8, rank)), shaped((m, rank))),
        (ids, inverse, sketch, top, top_other, low, low_other),
        [whole_smem] + [whole_vmem] * 2 + [columns(2 * n8)] * 4,
        (columns(rank), fixed(8, rank), fixed(m, rank)), tiles,
        scratch=[pltpu.VMEM((rank, tn), f32)], flops=6 * n * rank * rank, moved=12 * n * rank)
    squares = squares + swap(squares, "col", 1)
    w1, w2, w3 = swaps(squares, "col", 2)
    squares = (squares + w1) + (w2 + w3)
    weights_new, factor_new = call(
        functools.partial(weights_kernel, n_total, step_rate * math.sqrt(m_total / rank)),
        (shaped((m, n)), shaped((n, rank))), (squares, basis, right, weights),
        [whole_vmem] * 2 + [columns(rank), columns(m)],
        (columns(m), pl.BlockSpec((tn, rank), lambda i, *_: (i, 0))), tiles,
        scratch=[pltpu.VMEM((m, rank), bf16)] * 2, flops=6 * m * n * rank, moved=6 * m * n)
    momentum_new = call(
        functools.partial(momentum_kernel, late), shaped((m, n)),
        (ids, own_all, other_all, second_by_y, second_by_x, basis, right, moment),
        [pick(3), pick(3), columns(quarter), columns(quarter), fixed(m, rank), columns(rank), columns(m)],
        columns(m), tiles, scratch=[pltpu.VMEM((m, rank), bf16)],
        flops=2 * m * n * (tokens // 2 + rank), moved=8 * m * n, prefetch=1, aliases={7: 0})
    return (weights_new, momentum_new, factor_new)


def solution(mesh):
    n_row, n_col = mesh.shape["row"], mesh.shape["col"]
    fast = (n_row, n_col) == (4, 8)
    body = plane if fast else general

    def whole(inputs, out_grads, weights, momentum, right_factor):
        m_total, n_total = weights.shape
        return jax.shard_map(
            functools.partial(body, n_total, m_total),
            mesh=mesh,
            in_specs=(P("row", "col"), P("col", "row"), P("row", "col"), P("row", "col"), P("col", None)),
            out_specs=(P("row", "col"), P("row", "col"), P("col", None)),
            check_vma=False,
        )(inputs, out_grads, weights, momentum, right_factor)

    return whole
```
